256 devices in a mesh: panel: 16 (over y_hi, z), dir: 8 (over x, core), freq: 2 (over y_lo).
Axes of the slice: x: 4, y: 4 (y_hi: 2, y_lo: 2; y = y_hi * 2 + y_lo), z: 8, core: 2. Of those that a mesh axis runs over, the one named last changes fastest.
Arguments:
- sources: bfloat16 [4, 2, 64, 65536], P('freq', None, None, 'panel'), may hold values from -0.046875 to 0.046875
- panel_geom: float32 [4, 65536], P(None, 'panel'), may hold values from -150 to 150, as said below
- drift_cot: float32 [4, 64], P('freq'), may hold values from -4 to 4
- freq_index: int32 [4], P('freq'), may hold values from 0 to 511
- heading_dir: int32 [64], replicated, may hold values from 0 to 4095
Outputs:
- source_grad: float32 [4, 2, 64, 65536], P('freq', None, None, ('panel', 'dir'))
- geom_grad: float32 [4, 65536], P(None, ('panel', 'dir'))
The draws below stay inside these ranges and needn't reach their ends.
Inputs may be any that keep to these rules, and one draw needn't show every extreme that they name: `panel_geom`: rows are panel centre x, y, z in metres, z at or below the water line, and panel area from 0.5 to 2.
All inputs are finite; a program needn't handle non-finite values.
Results may differ from the reference program's by a relative error of at most 0.00042.
Values may be sent and summed in bfloat16 or wider, within the bound.
A program may use at most 64 MiB of HBM per device.

```python
import math
import jax
import jax.numpy as jnp
from jax import lax

PANELS = 65536
ND = 4096
HEADINGS = 64
NWIN = 4
FREQS = 512


def draw_panel_geom(key, part):
    keys = jax.random.split(key, 5)
    count = PANELS
    xpos = jax.random.uniform(keys[0], (count,), jnp.float32, -150.0, 150.0)
    side = jax.random.randint(keys[1], (count,), 0, 2).astype(jnp.float32) * 70.0 - 35.0
    ypos = side + jax.random.uniform(keys[2], (count,), jnp.float32, -22.0, 22.0)
    zpos = jax.random.uniform(keys[3], (count,), jnp.float32, -20.0, 0.0)
    area = jnp.exp(jax.random.uniform(keys[4], (count,), jnp.float32, math.log(0.5), math.log(2.0)))
    return jnp.stack([xpos, ypos, zpos, area])


def plant(entries, rng, low, largest):
    shape = entries.shape
    place = [jax.random.randint(jax.random.fold_in(rng, axis), (), 0, shape[axis]) for axis in range(len(shape))]
    entries = entries.at[tuple(place)].set(low)
    longest = shape.index(max(shape))
    place[longest] = (place[longest] + 1) % shape[longest]
    return entries.at[tuple(place)].set(largest)


def block_levels(stream_key, shape, shards, smallest, high):
    def one(axis_at, blocks):
        steps = jax.random.uniform(jax.random.fold_in(jax.random.fold_in(stream_key, 6), axis_at), (blocks,), jnp.float32, smallest / len(shards), high / len(shards))
        return jnp.repeat(jnp.exp(steps), shape[axis_at] // blocks).reshape((-1,) + (1,) * (len(shape) - axis_at - 1))

    level = one(*shards[0])
    for cut in shards[1:]:
        level = level * one(*cut)
    return level


def scatter_about(key, extent, spread, bound, cuts=(), kind=jnp.bfloat16):
    result = jax.random.normal(key, extent, jnp.float32) * spread
    if len(cuts) > 0:
        result = block_levels(key, extent, cuts, -0.22, 0.18) * result
    return jnp.clip(result, min=-bound, max=bound).astype(kind)


def setup_inputs(seed: int = 0) -> dict:
    key_of = jax.random.split(jax.random.key(seed), 6)
    sources = scatter_about(key_of[0], (NWIN, 2, HEADINGS, PANELS), (PANELS // 4) ** -0.5, 0.046875, ((0, 2), (3, 16)))
    panel_geom = draw_panel_geom(jax.random.fold_in(key_of[5], 71), 0)
    drift_cot = scatter_about(key_of[2], (NWIN, HEADINGS), 1.0, 4.0, ((0, 2),), jnp.float32)
    freq_index = plant(jax.random.randint(key_of[3], (NWIN,), 0, FREQS), jax.random.fold_in(key_of[3], 1), 0, FREQS - 1).astype(jnp.int32)
    heading_dir = plant(jax.random.randint(key_of[4], (HEADINGS,), 0, ND), jax.random.fold_in(key_of[4], 1), 0, ND - 1).astype(jnp.int32)
    return {"sources": sources, "panel_geom": panel_geom, "drift_cot": drift_cot, "freq_index": freq_index, "heading_dir": heading_dir}


gravity = 9.81
omega_low = 0.6
omega_span = 0.8
drift_gain = 5.0
cross_gain = 0.5
shape_scale = 100.0

def wave_numbers(freq_index):
    omega = omega_low + omega_span * freq_index.astype(jnp.float32) / FREQS
    return omega * omega / gravity

def direction_angles(dir_ids):
    return dir_ids.astype(jnp.float32) * (2.0 * math.pi / ND)

def phase_terms(geometry, wave, angles):
    amplitude = geometry[3] * jnp.exp(wave * geometry[2])
    phase = wave * (geometry[0][:, None] * jnp.cos(angles)[None, :] + geometry[1][:, None] * jnp.sin(angles)[None, :])
    return (amplitude[:, None] * jnp.cos(phase), -amplitude[:, None] * jnp.sin(phase))

def kochin_block(sig, geometry, wave, dir_ids):
    heads = sig.shape[1]
    real, imag = phase_terms(geometry, wave, direction_angles(dir_ids))
    width = real.shape[1]
    phases = jnp.concatenate([real, imag], 1).astype(jnp.bfloat16)
    prod = jnp.dot(sig.reshape(2 * heads, sig.shape[2]), phases, preferred_element_type=jnp.float32)
    kreal = prod[:heads, :width] - prod[heads:, width:]
    kimag = prod[:heads, width:] + prod[heads:, :width]
    return jnp.stack([kreal, kimag])

def cotangent(kochin, wave, dir_ids, weight, heading_dir):
    angles = direction_angles(dir_ids)
    slope = -drift_gain * wave / math.sqrt(ND)
    beta = direction_angles(heading_dir)
    hit = (dir_ids[None, :] == heading_dir[:, None]).astype(jnp.float32)
    along = 2.0 * slope * jnp.cos(angles)[None, :]
    real_part = weight[:, None] * (along * kochin[0] - cross_gain * jnp.cos(beta)[:, None] * hit)
    imag_part = weight[:, None] * (along * kochin[1])
    return jnp.stack([real_part, imag_part]).astype(jnp.bfloat16)

def backward_block(sig, geometry, wave, dir_ids, cot):
    heads = sig.shape[1]
    angles = direction_angles(dir_ids)
    real, imag = phase_terms(geometry, wave, angles)
    width = real.shape[1]
    phases = jnp.concatenate([real, imag], 1).astype(jnp.bfloat16)
    mixed = jnp.concatenate([jnp.concatenate([cot[0], cot[1]], 1), jnp.concatenate([cot[1], -cot[0]], 1)], 0)
    flat = sig.reshape(2 * heads, sig.shape[2])
    dsig = jnp.dot(mixed, phases.T, preferred_element_type=jnp.float32)
    dphase = jnp.dot(flat.T, mixed, preferred_element_type=jnp.float32)
    d_real = dphase[:, :width]
    d_imag = dphase[:, width:]
    twist = d_real * imag - d_imag * real
    swell = d_real * real + d_imag * imag
    shape = jnp.stack([wave * lax.optimization_barrier(jnp.sum(twist * jnp.cos(angles)[None, :], 1)), wave * lax.optimization_barrier(jnp.sum(twist * jnp.sin(angles)[None, :], 1)), wave * lax.optimization_barrier(jnp.sum(swell, 1)), lax.optimization_barrier(jnp.sum(swell, 1)) / geometry[3]])
    return (dsig, shape)

def reference(sources, panel_geom, drift_cot, freq_index, heading_dir):
    waves = wave_numbers(freq_index)
    dir_ids = jnp.arange(ND, dtype=jnp.int32)
    rows = min(PANELS, 4096)
    count = PANELS // rows
    geo_blocks = panel_geom.reshape(4, count, rows).transpose(1, 0, 2)
    grads = []
    shape_total = jnp.zeros((4, PANELS), jnp.float32)
    for freq in range(NWIN):
        sig_blocks = sources[freq].reshape(2, HEADINGS, count, rows).transpose(2, 0, 1, 3)
        wave = waves[freq]

        def add_block(total, blk):
            return (total + kochin_block(blk[0], blk[1], wave, dir_ids), None)
        kochin, unused = lax.scan(add_block, jnp.zeros((2, HEADINGS, ND), jnp.float32), (sig_blocks, geo_blocks))
        cot = cotangent(kochin, wave, dir_ids, drift_cot[freq], heading_dir)

        def back_block(carry, blk):
            return (carry, backward_block(blk[0], blk[1], wave, dir_ids, cot))
        unused, outs = lax.scan(back_block, jnp.zeros((), jnp.float32), (sig_blocks, geo_blocks))
        dsig = outs[0].transpose(1, 0, 2).reshape(2, HEADINGS, PANELS)
        grads.append(dsig)
        shape_total = shape_total + outs[1].transpose(1, 0, 2).reshape(4, PANELS)
    return (jnp.stack(grads), shape_scale * shape_total)
```

```python
import functools
import math

import jax
import jax.numpy as jnp
import numpy as np
from jax import lax
from jax.experimental import pallas as pl
from jax.experimental.pallas import tpu as pltpu
from jax.sharding import PartitionSpec as P

ND = 4096
FREQS = 512
HALF = ND // 2

gravity = 9.81
omega_low = 0.6
omega_span = 0.8
drift_gain = 5.0
cross_gain = 0.5
shape_scale = 100.0

MESH = pl.DeviceIdType.MESH
F32 = jnp.float32
BF16 = jnp.bfloat16
ROUNDER = 1.5 * 2.0**23


def fit_even(values, degree):
    nodes = np.cos((2 * np.arange(400) + 1) * np.pi / 800)
    t = (nodes + 1) / 8
    cheb = np.polynomial.chebyshev.Chebyshev.fit(t, values(t), degree, domain=[0, 0.25])
    return [float(np.float32(c)) for c in cheb.convert(kind=np.polynomial.Polynomial).coef]


SIN_COEF = fit_even(lambda t: np.sinc(np.sqrt(t)) * np.pi, 4)
COS_COEF = fit_even(lambda t: np.cos(np.pi * np.sqrt(t)), 4)


def horner(coef, t):
    total = t * coef[-1] + coef[-2]
    for c in coef[-3::-1]:
        total = total * t + c
    return total


def half_angle(turns):
    r = turns - ((turns + ROUNDER) - ROUNDER)
    t = r * r
    return r * horner(SIN_COEF, t), horner(COS_COEF, t)


def kernel(
    sizes,
    src_hbm,
    geom_ref,
    cot_ref,
    fidx_ref,
    head_ref,
    table_ref,
    out_ref,
    geo_ref,
    src,
    vecs,
    ctab,
    stab,
    ef,
    eb,
    hpart,
    rsbuf,
    gall,
    lmat,
    lmat_t,
    dscr,
    ssend,
    sown,
    sbuf,
    xbuf,
    gsum,
    gbuf,
    src_sem,
    rs_send,
    rs_recv,
    ag_send,
    ag_recv,
    sib_send,
    sib_recv,
    x_send,
    x_recv,
    g_send,
    g_recv,
):
    npan, ndir, nfreq, nf, panels, block = sizes
    nx = ndir // 2
    dirs = HALF // ndir
    own = dirs // npan
    rows = 2 * own
    heads2 = src.shape[1]
    heads = heads2 // 2
    pi = lax.axis_index("panel")
    di = lax.axis_index("dir")
    fi = lax.axis_index("freq")
    x = di // 2
    core = di % 2

    copies = [pltpu.make_async_copy(src_hbm.at[f], src.at[f], src_sem.at[f]) for f in range(nf)]
    for c in copies:
        c.start()

    barrier = pltpu.get_barrier_semaphore()

    def greet_panel(o, carry):
        pl.semaphore_signal(barrier, inc=1, device_id={"panel": (pi + o) % npan}, device_id_type=MESH)
        return carry

    lax.fori_loop(1, npan, greet_panel, 0)
    for b in range(nfreq):

        def greet_dir(o, carry):
            pl.semaphore_signal(
                barrier,
                inc=1,
                device_id={"dir": (di + o) % ndir, "freq": (fi + b) % nfreq},
                device_id_type=MESH,
            )
            return carry

        lax.fori_loop(0 if b else 1, ndir, greet_dir, 0)

    for half in range(dirs // 128):
        row = di * (dirs // 128) + half
        at = pl.ds(half * 128, 128)
        ctab[at, :] = jnp.broadcast_to(table_ref[0, pl.ds(row, 1), :], (128, 128)).T
        stab[at, :] = jnp.broadcast_to(table_ref[1, pl.ds(row, 1), :], (128, 128)).T

    gsum[...] = jnp.zeros(gsum.shape, F32)
    for f in range(nf):
        omega = omega_low + omega_span * fidx_ref[f].astype(F32) / FREQS
        om = jnp.full((1, panels), omega, F32)
        k = om * om / gravity
        amp = geom_ref[3:4, :] * jnp.exp(k * geom_ref[2:3, :])
        vecs[f, 0:1, :] = k * geom_ref[0:1, :] * (0.5 / math.pi)
        vecs[f, 1:2, :] = k * geom_ref[1:2, :] * (0.5 / math.pi)
        vecs[f, 2:3, :] = amp
        vecs[f, 3:4, :] = -2.0 * amp
        vecs[f, 4:5, :] = k

    def forward(f):
        def step(b, carry):
            lanes = pl.ds(pl.multiple_of(b * block, block), block)

            def gen(g, inner):
                at = pl.ds(pl.multiple_of(g * own, own), own)
                ct = jnp.concatenate([ctab[at, :]] * (block // 128), axis=1)
                st = jnp.concatenate([stab[at, :]] * (block // 128), axis=1)
                turns = vecs[f, 0:1, lanes] * ct + vecs[f, 1:2, lanes] * st
                s, c = half_angle(turns)
                q = s * vecs[f, 3:4, lanes]
                re = vecs[f, 2:3, lanes] + q * s
                im = q * c
                base = pl.multiple_of(g * rows, rows)
                ef[f, pl.ds(base, own), lanes] = re
                ef[f, pl.ds(base + own, own), lanes] = im
                eb[f, pl.ds(base, own), lanes] = re.astype(BF16)
                eb[f, pl.ds(base + own, own), lanes] = im.astype(BF16)
                return inner

            lax.fori_loop(0, npan, gen, 0)
            hpart[f] += lax.dot_general(
                eb[f, :, lanes],
                src[f, :, lanes],
                (((1,), (1,)), ((), ())),
                preferred_element_type=F32,
            )
            return carry

        hpart[f] = jnp.zeros(hpart.shape[1:], F32)
        copies[f].wait()
        lax.fori_loop(0, panels // block, step, 0)

    def rs_copy(f, o):
        dest = (pi + o) % npan
        return pltpu.make_async_remote_copy(
            src_ref=hpart.at[f, pl.ds(pl.multiple_of(dest * rows, rows), rows)],
            dst_ref=rsbuf.at[f, o],
            send_sem=rs_send.at[f, o],
            recv_sem=rs_recv.at[f, o],
            device_id={"panel": dest},
            device_id_type=MESH,
        )

    def ag_copy(f, o):
        dest = (pi + o) % npan
        return pltpu.make_async_remote_copy(
            src_ref=gall.at[f, pi],
            dst_ref=gall.at[f, pi],
            send_sem=ag_send.at[f, o],
            recv_sem=ag_recv.at[f, o],
            device_id={"panel": dest},
            device_id_type=MESH,
        )

    def ag_arrival(f, o):
        origin = (pi - o + npan) % npan
        return pltpu.make_async_remote_copy(
            src_ref=gall.at[f, origin],
            dst_ref=gall.at[f, origin],
            send_sem=ag_send.at[f, o],
            recv_sem=ag_recv.at[f, o],
            device_id={"panel": origin},
            device_id_type=MESH,
        )

    def loop_over(lo, hi, fn):
        def step(o, carry):
            fn(o)
            return carry

        lax.fori_loop(lo, hi, step, 0)

    def cotangent(f):
        loop_over(1, npan, lambda o: rs_copy(f, o).wait_recv())
        total = hpart[f, pl.ds(pl.multiple_of(pi * rows, rows), rows), :]
        for o in range(1, npan):
            total = total + rsbuf[f, o]
        top = total[:own]
        low = pltpu.roll(total[own:], heads, 1)
        lane = lax.broadcasted_iota(jnp.int32, (own, heads2), 1)
        first = lane < heads
        sign = jnp.where(first, 1.0, -1.0)
        head = head_ref[...]
        sb, _ = half_angle(head.astype(F32) * (1.0 / ND))
        cosb = 1.0 - 2.0 * sb * sb
        ids = di * dirs + pi * own + lax.broadcasted_iota(jnp.int32, (own, heads2), 0)
        slope = vecs[f, 4:5, 0:heads2] * (-drift_gain) / math.sqrt(ND)
        along = 2.0 * slope * ctab[pl.ds(pl.multiple_of(pi * own, own), own), :] * sign
        weight = cot_ref[f : f + 1, :]
        pull = cross_gain * cosb
        hit = jnp.where((ids == head) & first, pull, 0.0)
        hit_far = jnp.where((ids + HALF == head) & first, pull, 0.0)
        near = weight * (along * (top - low) - hit)
        far = weight * (-along * (top + low) - hit_far)
        gall[f, pi] = jnp.concatenate([near, far], axis=1).astype(BF16)
        loop_over(1, npan, lambda o: ag_copy(f, o).start())

    def gather(f):
        loop_over(1, npan, lambda o: ag_arrival(f, o).wait_recv())

        def build(g, carry):
            near = gall[f, g, :, 0:heads2].astype(F32)
            far = gall[f, g, :, heads2:].astype(F32)
            top = jnp.concatenate([near, far], axis=1)
            low = jnp.concatenate([pltpu.roll(far, heads, 1), -pltpu.roll(near, heads, 1)], axis=1)
            both = jnp.concatenate([top, low], axis=0)
            base = pl.multiple_of(g * rows, rows)
            lmat[f, pl.ds(base, rows), :] = both.astype(BF16)
            return carry

        lax.fori_loop(0, npan, build, 0)
        for part in range(2 * dirs // 128):
            at = pl.ds(part * 128, 128)
            lmat_t[f, :, at] = lmat[f, at, :].astype(F32).T.astype(BF16)

    sub = 256

    def backward(f, xdest, side, dst):
        j = xdest * 2 + side

        def step(n, carry):
            lanes = pl.ds(pl.multiple_of(j * block + n * sub, sub), sub)
            w = src[f, :, lanes]
            both = jnp.dot(lmat_t[f], eb[f, :, lanes], preferred_element_type=F32)
            dst[:, pl.ds(pl.multiple_of(n * sub, sub), sub)] = both[:heads2] + both[heads2:]
            dscr[...] = jnp.dot(lmat[f], jnp.concatenate([w, w], axis=0), preferred_element_type=F32)

            def shape(g, acc):
                base = pl.multiple_of(g * rows, rows)
                at = pl.ds(pl.multiple_of(g * own, own), own)
                ct = jnp.concatenate([ctab[at, :]] * (sub // 128), axis=1)
                st = jnp.concatenate([stab[at, :]] * (sub // 128), axis=1)
                u = dscr[pl.ds(base, own), :]
                v = dscr[pl.ds(base + own, own), :]
                re = ef[f, pl.ds(base, own), lanes]
                im = ef[f, pl.ds(base + own, own), lanes]
                twist = u * im - v * re
                swell = u * re + v * im
                terms = (twist * ct, twist * st, swell)
                return tuple(
                    a + sum(t[8 * i : 8 * i + 8] for i in range(own // 8))
                    for a, t in zip(acc, terms)
                )

            zero = jnp.zeros((8, sub), F32)
            qc, qs, rs = lax.fori_loop(0, npan, shape, (zero, zero, zero))
            k = vecs[f, 4:5, lanes]
            qc = k * jnp.sum(qc, axis=0, keepdims=True)
            qs = k * jnp.sum(qs, axis=0, keepdims=True)
            rs = jnp.sum(rs, axis=0, keepdims=True)
            here = pl.ds(pl.multiple_of(n * sub, sub), sub)
            for r, value in enumerate((qc, qs, k * rs, rs)):
                gsum[j, r : r + 1, here] += value
            return carry

        lax.fori_loop(0, block // sub, step, 0)

    xp = (x + 1) % nx
    xm = (x + nx - 1) % nx
    x2 = (x + 2) % nx
    order = (x2, xp, xm, x)

    def sib_copy(f, n):
        return pltpu.make_async_remote_copy(
            src_ref=ssend.at[f, n],
            dst_ref=sbuf.at[f, n],
            send_sem=sib_send.at[f, n],
            recv_sem=sib_recv.at[f, n],
            device_id={"dir": x * 2 + (1 - core)},
            device_id_type=MESH,
        )

    upper, lower = pl.ds(0, heads), pl.ds(heads, heads)
    messages = (
        (0, upper, xp),
        (0, lower, xm),
        (1, lower, xp),
        (1, upper, xp),
        (2, upper, xm),
        (2, lower, xm),
    )

    def x_copy(f, m):
        n, part, to = messages[m]
        return pltpu.make_async_remote_copy(
            src_ref=sown.at[f, n, part],
            dst_ref=xbuf.at[f, m],
            send_sem=x_send.at[f, m],
            recv_sem=x_recv.at[f, m],
            device_id={"dir": to * 2 + core},
            device_id_type=MESH,
        )

    def to_sibling(f, n):
        backward(f, order[n], 1 - core, ssend.at[f, n])
        sib_copy(f, n).start()

    def keep(f, n):
        backward(f, order[n], core, sown.at[f, n])

    def join(f, n):
        sib_copy(f, n).wait_recv()
        sown[f, n] += sbuf[f, n]

    def reverse(f):
        to_sibling(f, 0)
        keep(f, 0)
        to_sibling(f, 1)
        join(f, 0)
        x_copy(f, 0).start()
        x_copy(f, 1).start()
        keep(f, 1)
        to_sibling(f, 2)
        join(f, 1)
        x_copy(f, 2).start()
        keep(f, 2)
        to_sibling(f, 3)
        join(f, 2)
        x_copy(f, 4).start()
        keep(f, 3)

    def relay(f):
        x_copy(f, 0).wait_recv()
        sown[f, 1, upper] += xbuf[f, 0]
        x_copy(f, 3).start()
        x_copy(f, 1).wait_recv()
        sown[f, 2, lower] += xbuf[f, 1]
        x_copy(f, 5).start()

    def finish(f):
        sib_copy(f, 3).wait_recv()
        for m in (2, 3, 4, 5):
            x_copy(f, m).wait_recv()
        total = sown[f, 3] + sbuf[f, 3]
        out_ref[f, upper] = total[:heads] + xbuf[f, 3] + xbuf[f, 4]
        out_ref[f, lower] = total[heads:] + xbuf[f, 2] + xbuf[f, 5]

    def g_copy(b, o):
        to = (di + o) % ndir
        return pltpu.make_async_remote_copy(
            src_ref=gsum.at[to],
            dst_ref=gbuf.at[b, o],
            send_sem=g_send.at[b, o],
            recv_sem=g_recv.at[b, o],
            device_id={"dir": to, "freq": (fi + b) % nfreq},
            device_id_type=MESH,
        )

    for f in range(nf):
        forward(f)
        if f == 0:
            pl.semaphore_wait(barrier, npan - 1 + nfreq * ndir - 1)
        loop_over(1, npan, lambda o: rs_copy(f, o).start())
    for f in range(nf):
        cotangent(f)
    gather(0)
    reverse(0)
    gather(1)
    relay(0)
    reverse(1)
    for b in range(nfreq):
        loop_over(0 if b else 1, ndir, lambda o: g_copy(b, o).start())
    relay(1)
    finish(0)
    for b in range(nfreq):
        loop_over(0 if b else 1, ndir, lambda o: g_copy(b, o).wait_recv())
    total = gsum[di]
    for b in range(nfreq):
        for o in range(0 if b else 1, ndir):
            total = total + gbuf[b, o]
    area = geom_ref[3:4, pl.ds(pl.multiple_of(di * block, block), block)]
    geo_ref[0:3, :] = shape_scale * total[0:3]
    geo_ref[3:4, :] = shape_scale * (total[3:4] / area)
    finish(1)

    for f in range(nf):
        loop_over(1, npan, lambda o: rs_copy(f, o).wait_send())
        loop_over(1, npan, lambda o: ag_copy(f, o).wait_send())
        for n in range(4):
            sib_copy(f, n).wait_send()
        for m in range(6):
            x_copy(f, m).wait_send()
    for b in range(nfreq):
        loop_over(0 if b else 1, ndir, lambda o: g_copy(b, o).wait_send())


def direction_table():
    angle = np.arange(HALF, dtype=np.float64) * (2.0 * np.pi / ND)
    return np.stack([np.cos(angle), np.sin(angle)]).astype(np.float32).reshape(2, HALF // 128, 128)


def solution(mesh):
    npan, ndir, nfreq = (mesh.shape[a] for a in ("panel", "dir", "freq"))

    def body(sources, panel_geom, drift_cot, freq_index, heading_dir):
        nf, parts, heads, panels = sources.shape
        block = panels // ndir
        dirs = HALF // ndir
        own = dirs // npan
        heads2 = 2 * heads
        sizes = (npan, ndir, nfreq, nf, panels, block)
        dma = pltpu.SemaphoreType.DMA
        vmem = pltpu.VMEM
        out, geo = pl.pallas_call(
            functools.partial(kernel, sizes),
            out_shape=(
                jax.ShapeDtypeStruct((nf, heads2, block), F32),
                jax.ShapeDtypeStruct((4, block), F32),
            ),
            in_specs=[
                pl.BlockSpec(memory_space=pl.ANY),
                pl.BlockSpec(memory_space=vmem),
                pl.BlockSpec(memory_space=vmem),
                pl.BlockSpec(memory_space=pltpu.SMEM),
                pl.BlockSpec(memory_space=vmem),
                pl.BlockSpec(memory_space=vmem),
            ],
            out_specs=(pl.BlockSpec(memory_space=vmem), pl.BlockSpec(memory_space=vmem)),
            scratch_shapes=[
                vmem((nf, heads2, panels), BF16),
                vmem((nf, 8, panels), F32),
                vmem((dirs, 128), F32),
                vmem((dirs, 128), F32),
                vmem((nf, 2 * dirs, panels), F32),
                vmem((nf, 2 * dirs, panels), BF16),
                vmem((nf, 2 * dirs, heads2), F32),
                vmem((nf, npan, 2 * own, heads2), F32),
                vmem((nf, npan, own, 2 * heads2), BF16),
                vmem((nf, 2 * dirs, 2 * heads2), BF16),
                vmem((nf, 2 * heads2, 2 * dirs), BF16),
                vmem((2 * dirs, 256), F32),
                vmem((nf, 4, heads2, block), F32),
                vmem((nf, 4, heads2, block), F32),
                vmem((nf, 4, heads2, block), F32),
                vmem((nf, 6, heads, block), F32),
                vmem((ndir, 8, block), F32),
                vmem((nfreq, ndir, 8, block), F32),
                dma((nf,)),
                dma((nf, npan)),
                dma((nf, npan)),
                dma((nf, npan)),
                dma((nf, npan)),
                dma((nf, 4)),
                dma((nf, 4)),
                dma((nf, 6)),
                dma((nf, 6)),
                dma((nfreq, ndir)),
                dma((nfreq, ndir)),
            ],
            compiler_params=pltpu.CompilerParams(
                collective_id=0, has_side_effects=True, vmem_limit_bytes=60 * 1024 * 1024
            ),
        )(
            sources.reshape(nf, heads2, panels),
            panel_geom,
            jnp.concatenate([drift_cot, drift_cot], axis=1),
            freq_index,
            jnp.concatenate([heading_dir, heading_dir]).reshape(1, heads2),
            jnp.asarray(direction_table()),
        )
        return out.reshape(nf, parts, heads, block), geo

    return jax.shard_map(
        body,
        mesh=mesh,
        in_specs=(
            P("freq", None, None, "panel"),
            P(None, "panel"),
            P("freq", None),
            P("freq"),
            P(),
        ),
        out_specs=(P("freq", None, None, ("panel", "dir")), P(None, ("panel", "dir"))),
        check_vma=False,
    )
```

```python
import functools
import math

import jax
import jax.numpy as jnp
import numpy as np
from jax import lax
from jax.experimental import pallas as pl
from jax.experimental.pallas import tpu as pltpu
from jax.sharding import PartitionSpec as P

ND = 4096
FREQS = 512
HALF = ND // 2

gravity = 9.81
omega_low = 0.6
omega_span = 0.8
drift_gain = 5.0
cross_gain = 0.5
shape_scale = 100.0

MESH = pl.DeviceIdType.MESH
F32 = jnp.float32
BF16 = jnp.bfloat16
ROUNDER = 1.5 * 2.0**23


def fit_even(values, degree):
    nodes = np.cos((2 * np.arange(400) + 1) * np.pi / 800)
    t = (nodes + 1) / 8
    cheb = np.polynomial.chebyshev.Chebyshev.fit(t, values(t), degree, domain=[0, 0.25])
    return [float(np.float32(c)) for c in cheb.convert(kind=np.polynomial.Polynomial).coef]


SIN_COEF = fit_even(lambda t: np.sinc(np.sqrt(t)) * np.pi, 4)
COS_COEF = fit_even(lambda t: np.cos(np.pi * np.sqrt(t)), 4)


def horner(coef, t):
    total = t * coef[-1] + coef[-2]
    for c in coef[-3::-1]:
        total = total * t + c
    return total


def half_angle(turns):
    r = turns - ((turns + ROUNDER) - ROUNDER)
    t = r * r
    return r * horner(SIN_COEF, t), horner(COS_COEF, t)


def kernel(
    sizes,
    src_hbm,
    geom_ref,
    cot_ref,
    fidx_ref,
    head_ref,
    table_ref,
    out_ref,
    geo_ref,
    src,
    vecs,
    ctab,
    stab,
    ef,
    eb,
    hpart,
    rsbuf,
    gall,
    lmat,
    lmat_t,
    dscr,
    ssend,
    sown,
    sbuf,
    qsend,
    qrecv,
    msend,
    mrecv,
    gsum,
    gbuf,
    src_sem,
    rs_send,
    rs_recv,
    ag_send,
    ag_recv,
    sib_send,
    sib_recv,
    x_send,
    x_recv,
    g_send,
    g_recv,
):
    npan, ndir, nfreq, nf, panels, block = sizes
    nx = ndir // 2
    dirs = HALF // ndir
    own = dirs // npan
    rows = 2 * own
    heads2 = src.shape[1]
    heads = heads2 // 2
    pi = lax.axis_index("panel")
    di = lax.axis_index("dir")
    fi = lax.axis_index("freq")
    x = di // 2
    core = di % 2

    copies = [pltpu.make_async_copy(src_hbm.at[f], src.at[f], src_sem.at[f]) for f in range(nf)]
    for c in copies:
        c.start()

    barrier = pltpu.get_barrier_semaphore()

    def greet_panel(o, carry):
        pl.semaphore_signal(barrier, inc=1, device_id={"panel": (pi + o) % npan}, device_id_type=MESH)
        return carry

    lax.fori_loop(1, npan, greet_panel, 0)
    for b in range(nfreq):

        def greet_dir(o, carry):
            pl.semaphore_signal(
                barrier,
                inc=1,
                device_id={"dir": (di + o) % ndir, "freq": (fi + b) % nfreq},
                device_id_type=MESH,
            )
            return carry

        lax.fori_loop(0 if b else 1, ndir, greet_dir, 0)

    for half in range(dirs // 128):
        row = di * (dirs // 128) + half
        at = pl.ds(half * 128, 128)
        ctab[at, :] = jnp.broadcast_to(table_ref[0, pl.ds(row, 1), :], (128, 128)).T
        stab[at, :] = jnp.broadcast_to(table_ref[1, pl.ds(row, 1), :], (128, 128)).T

    gsum[...] = jnp.zeros(gsum.shape, F32)
    for f in range(nf):
        omega = omega_low + omega_span * fidx_ref[f].astype(F32) / FREQS
        om = jnp.full((1, panels), omega, F32)
        k = om * om / gravity
        amp = geom_ref[3:4, :] * jnp.exp(k * geom_ref[2:3, :])
        vecs[f, 0:1, :] = k * geom_ref[0:1, :] * (0.5 / math.pi)
        vecs[f, 1:2, :] = k * geom_ref[1:2, :] * (0.5 / math.pi)
        vecs[f, 2:3, :] = amp
        vecs[f, 3:4, :] = -2.0 * amp
        vecs[f, 4:5, :] = k
        vecs[f, 5:6, :] = 1.0 / amp

    def forward(f):
        def step(b, carry):
            lanes = pl.ds(pl.multiple_of(b * block, block), block)

            for g in range(npan):
                at = pl.ds(g * own, own)
                ct = jnp.concatenate([ctab[at, :]] * (block // 128), axis=1)
                st = jnp.concatenate([stab[at, :]] * (block // 128), axis=1)
                turns = vecs[f, 0:1, lanes] * ct + vecs[f, 1:2, lanes] * st
                s, c = half_angle(turns)
                q = s * vecs[f, 3:4, lanes]
                re = vecs[f, 2:3, lanes] + q * s
                im = q * c
                base = g * rows
                ef[f, pl.ds(base, own), lanes] = re
                ef[f, pl.ds(base + own, own), lanes] = im
                eb[f, pl.ds(base, own), lanes] = re.astype(BF16)
                eb[f, pl.ds(base + own, own), lanes] = im.astype(BF16)
            hpart[f] += lax.dot_general(
                eb[f, :, lanes],
                src[f, :, lanes],
                (((1,), (1,)), ((), ())),
                preferred_element_type=F32,
            )
            return carry

        hpart[f] = jnp.zeros(hpart.shape[1:], F32)
        copies[f].wait()
        lax.fori_loop(0, panels // block, step, 0)

    def rs_copy(f, o):
        dest = (pi + o) % npan
        return pltpu.make_async_remote_copy(
            src_ref=hpart.at[f, pl.ds(pl.multiple_of(dest * rows, rows), rows)],
            dst_ref=rsbuf.at[f, o],
            send_sem=rs_send.at[f, o],
            recv_sem=rs_recv.at[f, o],
            device_id={"panel": dest},
            device_id_type=MESH,
        )

    def ag_copy(f, o):
        dest = (pi + o) % npan
        return pltpu.make_async_remote_copy(
            src_ref=gall.at[f, pi],
            dst_ref=gall.at[f, pi],
            send_sem=ag_send.at[f, o],
            recv_sem=ag_recv.at[f, o],
            device_id={"panel": dest},
            device_id_type=MESH,
        )

    def ag_arrival(f, o):
        origin = (pi - o + npan) % npan
        return pltpu.make_async_remote_copy(
            src_ref=gall.at[f, origin],
            dst_ref=gall.at[f, origin],
            send_sem=ag_send.at[f, o],
            recv_sem=ag_recv.at[f, o],
            device_id={"panel": origin},
            device_id_type=MESH,
        )

    def loop_over(lo, hi, fn):
        def step(o, carry):
            fn(o)
            return carry

        lax.fori_loop(lo, hi, step, 0)

    def cotangent(f):
        loop_over(1, npan, lambda o: rs_copy(f, o).wait_recv())
        total = hpart[f, pl.ds(pl.multiple_of(pi * rows, rows), rows), :]
        for o in range(1, npan):
            total = total + rsbuf[f, o]
        top = total[:own]
        low = pltpu.roll(total[own:], heads, 1)
        lane = lax.broadcasted_iota(jnp.int32, (own, heads2), 1)
        first = lane < heads
        sign = jnp.where(first, 1.0, -1.0)
        head = jnp.concatenate([head_ref[...]] * 2, axis=1)
        sb, _ = half_angle(head.astype(F32) * (1.0 / ND))
        cosb = 1.0 - 2.0 * sb * sb
        ids = di * dirs + pi * own + lax.broadcasted_iota(jnp.int32, (own, heads2), 0)
        slope = vecs[f, 4:5, 0:heads2] * (-drift_gain) / math.sqrt(ND)
        along = 2.0 * slope * ctab[pl.ds(pl.multiple_of(pi * own, own), own), :] * sign
        weight = jnp.concatenate([cot_ref[f : f + 1, :]] * 2, axis=1)
        pull = cross_gain * cosb
        hit = jnp.where((ids == head) & first, pull, 0.0)
        hit_far = jnp.where((ids + HALF == head) & first, pull, 0.0)
        near = weight * (along * (top - low) - hit)
        far = weight * (-along * (top + low) - hit_far)
        gall[f, pi] = jnp.concatenate([near, far], axis=1).astype(BF16)
        loop_over(1, npan, lambda o: ag_copy(f, o).start())

    def gather(f):
        loop_over(1, npan, lambda o: ag_arrival(f, o).wait_recv())

        for g in range(npan):
            near = gall[f, g, :, 0:heads2].astype(F32)
            far = gall[f, g, :, heads2:].astype(F32)
            top = jnp.concatenate([near, far], axis=1)
            low = jnp.concatenate([pltpu.roll(far, heads, 1), -pltpu.roll(near, heads, 1)], axis=1)
            both = jnp.concatenate([top, low], axis=0)
            lmat[f, pl.ds(g * rows, rows), :] = both.astype(BF16)
        for part in range(2 * dirs // 128):
            at = pl.ds(part * 128, 128)
            lmat_t[f, :, at] = lmat[f, at, :].astype(F32).T.astype(BF16)

    sub = 256

    def backward(f, xdest, side, dst):
        j = xdest * 2 + side

        def step(n, carry):
            lanes = pl.ds(pl.multiple_of(j * block + n * sub, sub), sub)
            w = src[f, :, lanes]
            both = jnp.dot(lmat_t[f], eb[f, :, lanes], preferred_element_type=F32)
            dst[:, pl.ds(pl.multiple_of(n * sub, sub), sub)] = both[:heads2] + both[heads2:]
            dscr[...] = jnp.dot(lmat[f], jnp.concatenate([w, w], axis=0), preferred_element_type=F32)

            zero = jnp.zeros((8, sub), F32)
            acc = (zero, zero, zero)
            for g in range(npan):
                base = g * rows
                at = pl.ds(g * own, own)
                ct = jnp.concatenate([ctab[at, :]] * (sub // 128), axis=1)
                st = jnp.concatenate([stab[at, :]] * (sub // 128), axis=1)
                u = dscr[pl.ds(base, own), :]
                v = dscr[pl.ds(base + own, own), :]
                re = ef[f, pl.ds(base, own), lanes]
                im = ef[f, pl.ds(base + own, own), lanes]
                twist = u * im - v * re
                swell = u * re + v * im
                terms = (twist * ct, twist * st, swell)
                acc = tuple(
                    a + sum(t[8 * i : 8 * i + 8] for i in range(own // 8))
                    for a, t in zip(acc, terms)
                )
            qc, qs, rs = acc
            k = vecs[f, 4:5, lanes]
            qc = k * jnp.sum(qc, axis=0, keepdims=True)
            qs = k * jnp.sum(qs, axis=0, keepdims=True)
            rs = jnp.sum(rs, axis=0, keepdims=True)
            here = pl.ds(pl.multiple_of(n * sub, sub), sub)
            for r, value in enumerate((qc, qs, k * rs, rs)):
                gsum[j, r : r + 1, here] += value
            return carry

        lax.fori_loop(0, block // sub, step, 0)

    xp = (x + 1) % nx
    xm = (x + nx - 1) % nx
    x2 = (x + 2) % nx
    order = (x2, xp, xm, x)

    def sib_copy(f, n):
        return pltpu.make_async_remote_copy(
            src_ref=ssend.at[f, n],
            dst_ref=sbuf.at[f, n],
            send_sem=sib_send.at[f, n],
            recv_sem=sib_recv.at[f, n],
            device_id={"dir": x * 2 + (1 - core)},
            device_id_type=MESH,
        )

    upper, lower = pl.ds(0, heads), pl.ds(heads, heads)
    messages = (
        (0, upper, xp),
        (0, lower, xm),
        (1, lower, xp),
        (1, upper, xp),
        (2, upper, xm),
        (2, lower, xm),
    )

    def x_copies(f, m):
        to = messages[m][2]
        return [
            pltpu.make_async_remote_copy(
                src_ref=out_at.at[f, m],
                dst_ref=in_at.at[f, m],
                send_sem=x_send.at[f, m, i],
                recv_sem=x_recv.at[f, m, i],
                device_id={"dir": to * 2 + core},
                device_id_type=MESH,
            )
            for i, (out_at, in_at) in enumerate(((qsend, qrecv), (msend, mrecv)))
        ]

    def block_lanes(n):
        return pl.ds(pl.multiple_of((order[n] * 2 + core) * block, block), block)

    lane = lax.broadcasted_iota(jnp.int32, (8, 128), 1)

    def x_start(f, m):
        n, part, _ = messages[m]
        value = sown[f, n, part] * vecs[f, 5:6, block_lanes(n)]
        top = jnp.maximum(jnp.max(jnp.abs(value), axis=1, keepdims=True), 1e-30)
        level = value * (32000.0 / top)
        level = (level + ROUNDER) - ROUNDER
        qsend[f, m] = level.astype(jnp.int32).astype(jnp.int16)
        unit = jnp.broadcast_to(top * (1.0 / 32000.0), (heads, 128))
        packed = unit[0:8]
        for i in range(1, heads // 8):
            packed = jnp.where(lane >= 16 * i, unit[8 * i : 8 * i + 8], packed)
        msend[f, m] = packed
        for c in x_copies(f, m):
            c.start()

    def x_read(f, m, n):
        level = qrecv[f, m].astype(jnp.int32).astype(F32)
        unit = mrecv[f, m]
        unit = jnp.concatenate(
            [
                jnp.broadcast_to(unit[:, 16 * i : 16 * i + 1], (8, block))
                for i in range(heads // 8)
            ],
            axis=0,
        )
        return level * unit * vecs[f, 2:3, block_lanes(n)]

    def x_wait(f, m):
        for c in x_copies(f, m):
            c.wait_recv()

    def to_sibling(f, n):
        backward(f, order[n], 1 - core, ssend.at[f, n])
        sib_copy(f, n).start()

    def keep(f, n):
        backward(f, order[n], core, sown.at[f, n])

    def join(f, n):
        sib_copy(f, n).wait_recv()
        sown[f, n] += sbuf[f, n]

    def reverse(f):
        to_sibling(f, 0)
        keep(f, 0)
        to_sibling(f, 1)
        join(f, 0)
        x_start(f, 0)
        x_start(f, 1)
        keep(f, 1)
        to_sibling(f, 2)
        join(f, 1)
        x_start(f, 2)
        keep(f, 2)
        to_sibling(f, 3)
        join(f, 2)
        x_start(f, 4)
        keep(f, 3)

    def relay(f):
        x_wait(f, 0)
        sown[f, 1, upper] += x_read(f, 0, 1)
        x_start(f, 3)
        x_wait(f, 1)
        sown[f, 2, lower] += x_read(f, 1, 2)
        x_start(f, 5)

    def finish(f):
        sib_copy(f, 3).wait_recv()
        for m in (2, 4, 3, 5):
            x_wait(f, m)
        total = sown[f, 3] + sbuf[f, 3]
        out_ref[f, upper] = total[:heads] + x_read(f, 3, 3) + x_read(f, 4, 3)
        out_ref[f, lower] = total[heads:] + x_read(f, 2, 3) + x_read(f, 5, 3)

    def g_copy(b, o):
        to = (di + o) % ndir
        return pltpu.make_async_remote_copy(
            src_ref=gsum.at[to],
            dst_ref=gbuf.at[b, o],
            send_sem=g_send.at[b, o],
            recv_sem=g_recv.at[b, o],
            device_id={"dir": to, "freq": (fi + b) % nfreq},
            device_id_type=MESH,
        )

    for f in range(nf):
        forward(f)
        if f == 0:
            pl.semaphore_wait(barrier, npan - 1 + nfreq * ndir - 1)
        loop_over(1, npan, lambda o: rs_copy(f, o).start())
    for f in range(nf):
        cotangent(f)
    gather(0)
    reverse(0)
    gather(1)
    relay(0)
    reverse(1)
    for b in range(nfreq):
        loop_over(0 if b else 1, ndir, lambda o: g_copy(b, o).start())
    relay(1)
    finish(0)
    for b in range(nfreq):
        loop_over(0 if b else 1, ndir, lambda o: g_copy(b, o).wait_recv())
    total = gsum[di]
    for b in range(nfreq):
        for o in range(0 if b else 1, ndir):
            total = total + gbuf[b, o]
    area = geom_ref[3:4, pl.ds(pl.multiple_of(di * block, block), block)]
    geo_ref[0:3, :] = shape_scale * total[0:3]
    geo_ref[3:4, :] = shape_scale * (total[3:4] / area)
    finish(1)

    for f in range(nf):
        loop_over(1, npan, lambda o: rs_copy(f, o).wait_send())
        loop_over(1, npan, lambda o: ag_copy(f, o).wait_send())
        for n in range(4):
            sib_copy(f, n).wait_send()
        for m in range(6):
            for c in x_copies(f, m):
                c.wait_send()
    for b in range(nfreq):
        loop_over(0 if b else 1, ndir, lambda o: g_copy(b, o).wait_send())


def direction_table():
    angle = np.arange(HALF, dtype=np.float64) * (2.0 * np.pi / ND)
    return np.stack([np.cos(angle), np.sin(angle)]).astype(np.float32).reshape(2, HALF // 128, 128)


def solution(mesh):
    npan, ndir, nfreq = (mesh.shape[a] for a in ("panel", "dir", "freq"))

    def body(sources, panel_geom, drift_cot, freq_index, heading_dir):
        nf, parts, heads, panels = sources.shape
        block = panels // ndir
        dirs = HALF // ndir
        own = dirs // npan
        heads2 = 2 * heads
        sizes = (npan, ndir, nfreq, nf, panels, block)
        dma = pltpu.SemaphoreType.DMA
        vmem = pltpu.VMEM
        out, geo = pl.pallas_call(
            functools.partial(kernel, sizes),
            out_shape=(
                jax.ShapeDtypeStruct((nf, heads2, block), F32),
                jax.ShapeDtypeStruct((4, block), F32),
            ),
            in_specs=[
                pl.BlockSpec(memory_space=pl.ANY),
                pl.BlockSpec(memory_space=vmem),
                pl.BlockSpec(memory_space=vmem),
                pl.BlockSpec(memory_space=pltpu.SMEM),
                pl.BlockSpec(memory_space=vmem),
                pl.BlockSpec(memory_space=vmem),
            ],
            out_specs=(pl.BlockSpec(memory_space=vmem), pl.BlockSpec(memory_space=vmem)),
            scratch_shapes=[
                vmem((nf, heads2, panels), BF16),
                vmem((nf, 8, panels), F32),
                vmem((dirs, 128), F32),
                vmem((dirs, 128), F32),
                vmem((nf, 2 * dirs, panels), F32),
                vmem((nf, 2 * dirs, panels), BF16),
                vmem((nf, 2 * dirs, heads2), F32),
                vmem((nf, npan, 2 * own, heads2), F32),
                vmem((nf, npan, own, 2 * heads2), BF16),
                vmem((nf, 2 * dirs, 2 * heads2), BF16),
                vmem((nf, 2 * heads2, 2 * dirs), BF16),
                vmem((2 * dirs, 256), F32),
                vmem((nf, 4, heads2, block), F32),
                vmem((nf, 4, heads2, block), F32),
                vmem((nf, 4, heads2, block), F32),
                vmem((nf, 6, heads, block), jnp.int16),
                vmem((nf, 6, heads, block), jnp.int16),
                vmem((nf, 6, 8, 128), F32),
                vmem((nf, 6, 8, 128), F32),
                vmem((ndir, 8, block), F32),
                vmem((nfreq, ndir, 8, block), F32),
                dma((nf,)),
                dma((nf, npan)),
                dma((nf, npan)),
                dma((nf, npan)),
                dma((nf, npan)),
                dma((nf, 4)),
                dma((nf, 4)),
                dma((nf, 6, 2)),
                dma((nf, 6, 2)),
                dma((nfreq, ndir)),
                dma((nfreq, ndir)),
            ],
            compiler_params=pltpu.CompilerParams(
                collective_id=0, has_side_effects=True, vmem_limit_bytes=60 * 1024 * 1024
            ),
        )(
            sources.reshape(nf, heads2, panels),
            panel_geom,
            drift_cot,
            freq_index,
            heading_dir.reshape(1, heads),
            jnp.asarray(direction_table()),
        )
        return out.reshape(nf, parts, heads, block), geo

    return jax.shard_map(
        body,
        mesh=mesh,
        in_specs=(
            P("freq", None, None, "panel"),
            P(None, "panel"),
            P("freq", None),
            P("freq"),
            P(),
        ),
        out_specs=(P("freq", None, None, ("panel", "dir")), P(None, ("panel", "dir"))),
        check_vma=False,
    )
```

```python
import functools
import math

import jax
import jax.numpy as jnp
import numpy as np
from jax import lax
from jax.experimental import pallas as pl
from jax.experimental.pallas import tpu as pltpu
from jax.sharding import PartitionSpec as P

ND = 4096
FREQS = 512
HALF = ND // 2

gravity = 9.81
omega_low = 0.6
omega_span = 0.8
drift_gain = 5.0
cross_gain = 0.5
shape_scale = 100.0

MESH = pl.DeviceIdType.MESH
F32 = jnp.float32
BF16 = jnp.bfloat16
ROUNDER = 1.5 * 2.0**23


def fit_even(values, degree):
    nodes = np.cos((2 * np.arange(400) + 1) * np.pi / 800)
    t = (nodes + 1) / 8
    cheb = np.polynomial.chebyshev.Chebyshev.fit(t, values(t), degree, domain=[0, 0.25])
    return [float(np.float32(c)) for c in cheb.convert(kind=np.polynomial.Polynomial).coef]


SIN_COEF = fit_even(lambda t: np.sinc(np.sqrt(t)) * np.pi, 3)
COS_COEF = fit_even(lambda t: np.cos(np.pi * np.sqrt(t)), 4)


def horner(coef, t):
    total = t * coef[-1] + coef[-2]
    for c in coef[-3::-1]:
        total = total * t + c
    return total


def half_angle(turns):
    r = turns - ((turns + ROUNDER) - ROUNDER)
    t = r * r
    return r * horner(SIN_COEF, t), horner(COS_COEF, t)


def kernel(
    sizes,
    src_hbm,
    geom_ref,
    cot_ref,
    fidx_ref,
    head_ref,
    table_ref,
    out_ref,
    geo_ref,
    src,
    vecs,
    ctab,
    stab,
    ef,
    eb,
    hpart,
    pairbuf,
    rsbuf,
    gall,
    lmat,
    lmat_t,
    dscr,
    ssend,
    sown,
    sbuf,
    qsend,
    qrecv,
    msend,
    mrecv,
    gsum,
    gbuf,
    src_sem,
    pair_send,
    pair_recv,
    rs_send,
    rs_recv,
    ag_send,
    ag_recv,
    sib_send,
    sib_recv,
    x_send,
    x_recv,
    g_send,
    g_recv,
):
    npan, ndir, nfreq, nf, panels, block = sizes
    nx = ndir // 2
    dirs = HALF // ndir
    own = dirs // npan
    rows = 2 * own
    heads2 = src.shape[1]
    heads = heads2 // 2
    pi = lax.axis_index("panel")
    di = lax.axis_index("dir")
    fi = lax.axis_index("freq")
    x = di // 2
    core = di % 2

    copies = [pltpu.make_async_copy(src_hbm.at[f], src.at[f], src_sem.at[f]) for f in range(nf)]
    for c in copies:
        c.start()

    barrier = pltpu.get_barrier_semaphore()

    def greet_panel(o, carry):
        pl.semaphore_signal(barrier, inc=1, device_id={"panel": (pi + o) % npan}, device_id_type=MESH)
        return carry

    lax.fori_loop(1, npan, greet_panel, 0)
    for b in range(nfreq):

        def greet_dir(o, carry):
            pl.semaphore_signal(
                barrier,
                inc=1,
                device_id={"dir": (di + o) % ndir, "freq": (fi + b) % nfreq},
                device_id_type=MESH,
            )
            return carry

        lax.fori_loop(0 if b else 1, ndir, greet_dir, 0)

    for half in range(dirs // 128):
        row = di * (dirs // 128) + half
        at = pl.ds(half * 128, 128)
        ctab[at, :] = jnp.broadcast_to(table_ref[0, pl.ds(row, 1), :], (128, 128)).T
        stab[at, :] = jnp.broadcast_to(table_ref[1, pl.ds(row, 1), :], (128, 128)).T

    gsum[...] = jnp.zeros(gsum.shape, F32)
    def prepare(f):
        omega = omega_low + omega_span * fidx_ref[f].astype(F32) / FREQS
        om = jnp.full((1, panels), omega, F32)
        k = om * om / gravity
        amp = geom_ref[3:4, :] * jnp.exp(k * geom_ref[2:3, :])
        vecs[f, 0:1, :] = k * geom_ref[0:1, :] * (0.5 / math.pi)
        vecs[f, 1:2, :] = k * geom_ref[1:2, :] * (0.5 / math.pi)
        vecs[f, 2:3, :] = amp
        vecs[f, 3:4, :] = -2.0 * amp
        vecs[f, 4:5, :] = k
        vecs[f, 5:6, :] = 1.0 / amp

    def forward(f, lo, hi):
        some = pl.ds(lo * rows, (hi - lo) * rows)

        def step(b, carry):
            lanes = pl.ds(pl.multiple_of(b * block, block), block)

            for g in range(lo, hi):
                at = pl.ds(g * own, own)
                ct = jnp.concatenate([ctab[at, :]] * (block // 128), axis=1)
                st = jnp.concatenate([stab[at, :]] * (block // 128), axis=1)
                turns = vecs[f, 0:1, lanes] * ct + vecs[f, 1:2, lanes] * st
                s, c = half_angle(turns)
                q = s * vecs[f, 3:4, lanes]
                re = vecs[f, 2:3, lanes] + q * s
                im = q * c
                base = g * rows
                ef[f, pl.ds(base, own), lanes] = re
                ef[f, pl.ds(base + own, own), lanes] = im
                eb[f, pl.ds(base, own), lanes] = re.astype(BF16)
                eb[f, pl.ds(base + own, own), lanes] = im.astype(BF16)
            hpart[f, some] += lax.dot_general(
                eb[f, some, lanes],
                src[f, :, lanes],
                (((1,), (1,)), ((), ())),
                preferred_element_type=F32,
            )
            return carry

        hpart[f, some] = jnp.zeros(((hi - lo) * rows, heads2), F32)
        if lo == 0:
            prepare(f)
            copies[f].wait()
        lax.fori_loop(0, panels // block, step, 0)

    def loop_over(lo, hi, fn):
        def step(o, carry):
            fn(o)
            return carry

        lax.fori_loop(lo, hi, step, 0)

    ring = npan // 2
    side = pi // ring
    away = ring * rows

    def rs_size(f):
        return ring if f else npan

    def rs_copy(f, o):
        dest = side * ring + (pi + o) % ring if f else (pi + o) % npan
        return pltpu.make_async_remote_copy(
            src_ref=hpart.at[f, pl.ds(pl.multiple_of(dest * rows, rows), rows)],
            dst_ref=rsbuf.at[f, o],
            send_sem=rs_send.at[f, o],
            recv_sem=rs_recv.at[f, o],
            device_id={"panel": dest},
            device_id_type=MESH,
        )

    def pair_copy(f):
        other = pl.multiple_of((1 - side) * away, away)
        return pltpu.make_async_remote_copy(
            src_ref=hpart.at[f, pl.ds(other, away)],
            dst_ref=pairbuf.at[f],
            send_sem=pair_send.at[f],
            recv_sem=pair_recv.at[f],
            device_id={"panel": (pi + ring) % npan},
            device_id_type=MESH,
        )

    def spread(f):
        pair_copy(f).wait_recv()
        mine = pl.ds(pl.multiple_of(side * away, away), away)
        hpart[f, mine] += pairbuf[f]
        loop_over(1, ring, lambda o: rs_copy(f, o).start())

    def ag_copy(f, o):
        dest = (pi + o) % npan
        return pltpu.make_async_remote_copy(
            src_ref=gall.at[f, pi],
            dst_ref=gall.at[f, pi],
            send_sem=ag_send.at[f, o],
            recv_sem=ag_recv.at[f, o],
            device_id={"panel": dest},
            device_id_type=MESH,
        )

    def ag_arrival(f, o):
        origin = (pi - o + npan) % npan
        return pltpu.make_async_remote_copy(
            src_ref=gall.at[f, origin],
            dst_ref=gall.at[f, origin],
            send_sem=ag_send.at[f, o],
            recv_sem=ag_recv.at[f, o],
            device_id={"panel": origin},
            device_id_type=MESH,
        )

    def cotangent(f):
        loop_over(1, rs_size(f), lambda o: rs_copy(f, o).wait_recv())
        total = hpart[f, pl.ds(pl.multiple_of(pi * rows, rows), rows), :]
        for o in range(1, rs_size(f)):
            total = total + rsbuf[f, o]
        top = total[:own]
        low = pltpu.roll(total[own:], heads, 1)
        lane = lax.broadcasted_iota(jnp.int32, (own, heads2), 1)
        first = lane < heads
        sign = jnp.where(first, 1.0, -1.0)
        head = jnp.concatenate([head_ref[...]] * 2, axis=1)
        sb, _ = half_angle(head.astype(F32) * (1.0 / ND))
        cosb = 1.0 - 2.0 * sb * sb
        ids = di * dirs + pi * own + lax.broadcasted_iota(jnp.int32, (own, heads2), 0)
        slope = vecs[f, 4:5, 0:heads2] * (-drift_gain) / math.sqrt(ND)
        along = 2.0 * slope * ctab[pl.ds(pl.multiple_of(pi * own, own), own), :] * sign
        weight = jnp.concatenate([cot_ref[f : f + 1, :]] * 2, axis=1)
        pull = cross_gain * cosb
        hit = jnp.where((ids == head) & first, pull, 0.0)
        hit_far = jnp.where((ids + HALF == head) & first, pull, 0.0)
        near = weight * (along * (top - low) - hit)
        far = weight * (-along * (top + low) - hit_far)
        gall[f, pi] = jnp.concatenate([near, far], axis=1).astype(BF16)
        loop_over(1, npan, lambda o: ag_copy(f, o).start())

    def gather(f):
        loop_over(1, npan, lambda o: ag_arrival(f, o).wait_recv())

        for g in range(npan):
            near = gall[f, g, :, 0:heads2].astype(F32)
            far = gall[f, g, :, heads2:].astype(F32)
            top = jnp.concatenate([near, far], axis=1)
            low = jnp.concatenate([pltpu.roll(far, heads, 1), -pltpu.roll(near, heads, 1)], axis=1)
            both = jnp.concatenate([top, low], axis=0)
            lmat[f, pl.ds(g * rows, rows), :] = both.astype(BF16)
        for part in range(2 * dirs // 128):
            at = pl.ds(part * 128, 128)
            lmat_t[f, :, at] = lmat[f, at, :].astype(F32).T.astype(BF16)

    sub = 256

    def backward(f, xdest, column, dst):
        j = xdest * 2 + column

        def step(n, carry):
            lanes = pl.ds(pl.multiple_of(j * block + n * sub, sub), sub)
            w = src[f, :, lanes]
            both = jnp.dot(lmat_t[f], eb[f, :, lanes], preferred_element_type=F32)
            dst[:, pl.ds(pl.multiple_of(n * sub, sub), sub)] = both[:heads2] + both[heads2:]
            dscr[...] = jnp.dot(lmat[f], jnp.concatenate([w, w], axis=0), preferred_element_type=F32)

            zero = jnp.zeros((8, sub), F32)
            acc = (zero, zero, zero)
            for g in range(npan):
                base = g * rows
                at = pl.ds(g * own, own)
                ct = jnp.concatenate([ctab[at, :]] * (sub // 128), axis=1)
                st = jnp.concatenate([stab[at, :]] * (sub // 128), axis=1)
                u = dscr[pl.ds(base, own), :]
                v = dscr[pl.ds(base + own, own), :]
                re = ef[f, pl.ds(base, own), lanes]
                im = ef[f, pl.ds(base + own, own), lanes]
                twist = u * im - v * re
                swell = u * re + v * im
                terms = (twist * ct, twist * st, swell)
                acc = tuple(
                    a + sum(t[8 * i : 8 * i + 8] for i in range(own // 8))
                    for a, t in zip(acc, terms)
                )
            qc, qs, rs = acc
            k = vecs[f, 4:5, lanes]
            qc = k * jnp.sum(qc, axis=0, keepdims=True)
            qs = k * jnp.sum(qs, axis=0, keepdims=True)
            rs = jnp.sum(rs, axis=0, keepdims=True)
            for r, value in enumerate((qc, qs, k * rs, rs)):
                gsum[j, pl.ds(4 * n + r, 1), :] += value
            return carry

        lax.fori_loop(0, block // sub, step, 0)

    xp = (x + 1) % nx
    xm = (x + nx - 1) % nx
    x2 = (x + 2) % nx
    order = (x2, xp, xm, x)

    def sib_copy(f, n):
        return pltpu.make_async_remote_copy(
            src_ref=ssend.at[f, n],
            dst_ref=sbuf.at[f, n],
            send_sem=sib_send.at[f, n],
            recv_sem=sib_recv.at[f, n],
            device_id={"dir": x * 2 + (1 - core)},
            device_id_type=MESH,
        )

    upper, lower = pl.ds(0, heads), pl.ds(heads, heads)
    messages = (
        (0, upper, xp),
        (0, lower, xm),
        (1, lower, xp),
        (1, upper, xp),
        (2, upper, xm),
        (2, lower, xm),
    )

    def x_copies(f, m):
        to = messages[m][2]
        return [
            pltpu.make_async_remote_copy(
                src_ref=out_at.at[f, m],
                dst_ref=in_at.at[f, m],
                send_sem=x_send.at[f, m, i],
                recv_sem=x_recv.at[f, m, i],
                device_id={"dir": to * 2 + core},
                device_id_type=MESH,
            )
            for i, (out_at, in_at) in enumerate(((qsend, qrecv), (msend, mrecv)))
        ]

    def block_lanes(n):
        return pl.ds(pl.multiple_of((order[n] * 2 + core) * block, block), block)

    lane = lax.broadcasted_iota(jnp.int32, (8, 128), 1)

    def x_start(f, m):
        n, part, _ = messages[m]
        value = sown[f, n, part] * vecs[f, 5:6, block_lanes(n)]
        top = jnp.maximum(jnp.max(jnp.abs(value), axis=1, keepdims=True), 1e-30)
        level = value * (32000.0 / top)
        level = (level + ROUNDER) - ROUNDER
        qsend[f, m] = level.astype(jnp.int32).astype(jnp.int16)
        unit = jnp.broadcast_to(top * (1.0 / 32000.0), (heads, 128))
        packed = unit[0:8]
        for i in range(1, heads // 8):
            packed = jnp.where(lane >= 16 * i, unit[8 * i : 8 * i + 8], packed)
        msend[f, m] = packed
        for c in x_copies(f, m):
            c.start()

    def x_read(f, m, n):
        level = qrecv[f, m].astype(jnp.int32).astype(F32)
        unit = mrecv[f, m]
        unit = jnp.concatenate(
            [
                jnp.broadcast_to(unit[:, 16 * i : 16 * i + 1], (8, block))
                for i in range(heads // 8)
            ],
            axis=0,
        )
        return level * unit * vecs[f, 2:3, block_lanes(n)]

    def x_wait(f, m):
        for c in x_copies(f, m):
            c.wait_recv()

    def g_copy(b, o):
        to = (di + o) % ndir
        return pltpu.make_async_remote_copy(
            src_ref=gsum.at[to],
            dst_ref=gbuf.at[b, o],
            send_sem=g_send.at[b, o],
            recv_sem=g_recv.at[b, o],
            device_id={"dir": to, "freq": (fi + b) % nfreq},
            device_id_type=MESH,
        )

    def g_start(j, shifts):
        o = (j - di + ndir) % ndir
        for b in shifts:
            g_copy(b, o).start()

    def to_sibling(f, n):
        backward(f, order[n], 1 - core, ssend.at[f, n])
        sib_copy(f, n).start()
        if f == nf - 1:
            g_start(order[n] * 2 + (1 - core), range(nfreq))

    def keep(f, n):
        backward(f, order[n], core, sown.at[f, n])
        if f == nf - 1:
            g_start(order[n] * 2 + core, range(1 if n == 3 else 0, nfreq))

    def join(f, n):
        sib_copy(f, n).wait_recv()
        sown[f, n] += sbuf[f, n]

    def reverse(f, meanwhile=None):
        to_sibling(f, 0)
        keep(f, 0)
        to_sibling(f, 1)
        join(f, 0)
        x_start(f, 0)
        x_start(f, 1)
        keep(f, 1)
        to_sibling(f, 2)
        join(f, 1)
        x_start(f, 2)
        keep(f, 2)
        to_sibling(f, 3)
        join(f, 2)
        x_start(f, 4)
        if meanwhile:
            meanwhile()
        keep(f, 3)

    def relay(f):
        x_wait(f, 0)
        sown[f, 1, upper] += x_read(f, 0, 1)
        x_start(f, 3)
        x_wait(f, 1)
        sown[f, 2, lower] += x_read(f, 1, 2)
        x_start(f, 5)

    def finish(f):
        sib_copy(f, 3).wait_recv()
        for m in (2, 4, 3, 5):
            x_wait(f, m)
        total = sown[f, 3] + sbuf[f, 3]
        out_ref[f, upper] = total[:heads] + x_read(f, 3, 3) + x_read(f, 4, 3)
        out_ref[f, lower] = total[heads:] + x_read(f, 2, 3) + x_read(f, 5, 3)

    def send_sums(f, lo, hi):
        def one(dest):
            o = (dest - pi + npan) % npan

            @pl.when(o != 0)
            def _():
                rs_copy(f, o).start()

        loop_over(lo, hi, one)

    middle = npan // 2
    forward(0, 0, middle)
    pl.semaphore_wait(barrier, npan - 1 + nfreq * ndir - 1)
    send_sums(0, 0, middle)
    forward(0, middle, npan)
    send_sums(0, middle, npan)
    forward(1, 0, npan)
    pair_copy(1).start()
    cotangent(0)
    spread(1)
    cotangent(1)
    gather(0)
    reverse(0)
    gather(1)
    relay(0)
    reverse(1)
    relay(1)
    finish(0)
    for b in range(nfreq):
        loop_over(0 if b else 1, ndir, lambda o: g_copy(b, o).wait_recv())
    total = gsum[di]
    for b in range(nfreq):
        for o in range(0 if b else 1, ndir):
            total = total + gbuf[b, o]
    for n in range(block // sub):
        here = pl.ds(n * sub, sub)
        area = geom_ref[3:4, pl.ds(pl.multiple_of(di * block + n * sub, sub), sub)]
        geo_ref[0:3, here] = shape_scale * total[4 * n : 4 * n + 3]
        geo_ref[3:4, here] = shape_scale * (total[4 * n + 3 : 4 * n + 4] / area)
    finish(1)

    for f in range(nf):
        if f:
            pair_copy(f).wait_send()
        loop_over(1, rs_size(f), lambda o: rs_copy(f, o).wait_send())
        loop_over(1, npan, lambda o: ag_copy(f, o).wait_send())
        for n in range(4):
            sib_copy(f, n).wait_send()
        for m in range(6):
            for c in x_copies(f, m):
                c.wait_send()
    for b in range(nfreq):
        loop_over(0 if b else 1, ndir, lambda o: g_copy(b, o).wait_send())


def hand_on(out_in, geo_in, out_ref, geo_ref):
    out_ref[...] = out_in[...]
    geo_ref[...] = geo_in[...]


def direction_table():
    angle = np.arange(HALF, dtype=np.float64) * (2.0 * np.pi / ND)
    return np.stack([np.cos(angle), np.sin(angle)]).astype(np.float32).reshape(2, HALF // 128, 128)


def solution(mesh):
    npan, ndir, nfreq = (mesh.shape[a] for a in ("panel", "dir", "freq"))

    def body(sources, panel_geom, drift_cot, freq_index, heading_dir):
        nf, parts, heads, panels = sources.shape
        block = panels // ndir
        dirs = HALF // ndir
        own = dirs // npan
        heads2 = 2 * heads
        sizes = (npan, ndir, nfreq, nf, panels, block)
        dma = pltpu.SemaphoreType.DMA
        vmem = pltpu.VMEM
        out, geo = pl.pallas_call(
            functools.partial(kernel, sizes),
            out_shape=(
                jax.ShapeDtypeStruct((nf, heads2, block), F32),
                jax.ShapeDtypeStruct((4, block), F32),
            ),
            in_specs=[
                pl.BlockSpec(memory_space=pl.ANY),
                pl.BlockSpec(memory_space=vmem),
                pl.BlockSpec(memory_space=vmem),
                pl.BlockSpec(memory_space=pltpu.SMEM),
                pl.BlockSpec(memory_space=vmem),
                pl.BlockSpec(memory_space=vmem),
            ],
            out_specs=(pl.BlockSpec(memory_space=vmem), pl.BlockSpec(memory_space=vmem)),
            scratch_shapes=[
                vmem((nf, heads2, panels), BF16),
                vmem((nf, 8, panels), F32),
                vmem((dirs, 128), F32),
                vmem((dirs, 128), F32),
                vmem((nf, 2 * dirs, panels), F32),
                vmem((nf, 2 * dirs, panels), BF16),
                vmem((nf, 2 * dirs, heads2), F32),
                vmem((nf, dirs, heads2), F32),
                vmem((nf, npan, 2 * own, heads2), F32),
                vmem((nf, npan, own, 2 * heads2), BF16),
                vmem((nf, 2 * dirs, 2 * heads2), BF16),
                vmem((nf, 2 * heads2, 2 * dirs), BF16),
                vmem((2 * dirs, 256), F32),
                vmem((nf, 4, heads2, block), F32),
                vmem((nf, 4, heads2, block), F32),
                vmem((nf, 4, heads2, block), F32),
                vmem((nf, 6, heads, block), jnp.int16),
                vmem((nf, 6, heads, block), jnp.int16),
                vmem((nf, 6, 8, 128), F32),
                vmem((nf, 6, 8, 128), F32),
                vmem((ndir, 8, block // 2), F32),
                vmem((nfreq, ndir, 8, block // 2), F32),
                dma((nf,)),
                dma((nf,)),
                dma((nf,)),
                dma((nf, npan)),
                dma((nf, npan)),
                dma((nf, npan)),
                dma((nf, npan)),
                dma((nf, 4)),
                dma((nf, 4)),
                dma((nf, 6, 2)),
                dma((nf, 6, 2)),
                dma((nfreq, ndir)),
                dma((nfreq, ndir)),
            ],
            compiler_params=pltpu.CompilerParams(
                collective_id=0, has_side_effects=True, vmem_limit_bytes=60 * 1024 * 1024
            ),
        )(
            sources.reshape(nf, heads2, panels),
            panel_geom,
            drift_cot,
            freq_index,
            heading_dir.reshape(1, heads),
            jnp.asarray(direction_table()),
        )
        out, geo = pl.pallas_call(
            hand_on,
            out_shape=(
                jax.ShapeDtypeStruct(out.shape, F32),
                jax.ShapeDtypeStruct(geo.shape, F32),
            ),
        )(out, geo)
        return out.reshape(nf, parts, heads, block), geo

    return jax.shard_map(
        body,
        mesh=mesh,
        in_specs=(
            P("freq", None, None, "panel"),
            P(None, "panel"),
            P("freq", None),
            P("freq"),
            P(),
        ),
        out_specs=(P("freq", None, None, ("panel", "dir")), P(None, ("panel", "dir"))),
        check_vma=False,
    )
```

```python
import functools
import math

import jax
import jax.numpy as jnp
import numpy as np
from jax import lax
from jax.experimental import pallas as pl
from jax.experimental.pallas import tpu as pltpu
from jax.sharding import PartitionSpec as P

ND = 4096
FREQS = 512
HALF = ND // 2

gravity = 9.81
omega_low = 0.6
omega_span = 0.8
drift_gain = 5.0
cross_gain = 0.5
shape_scale = 100.0

MESH = pl.DeviceIdType.MESH
F32 = jnp.float32
BF16 = jnp.bfloat16
ROUNDER = 1.5 * 2.0**23


def fit_even(values, degree):
    nodes = np.cos((2 * np.arange(400) + 1) * np.pi / 800)
    t = (nodes + 1) / 8
    cheb = np.polynomial.chebyshev.Chebyshev.fit(t, values(t), degree, domain=[0, 0.25])
    return [float(np.float32(c)) for c in cheb.convert(kind=np.polynomial.Polynomial).coef]


SIN_COEF = fit_even(lambda t: np.sinc(np.sqrt(t)) * np.pi, 3)
COS_COEF = fit_even(lambda t: np.cos(np.pi * np.sqrt(t)), 3)


def horner(coef, t):
    total = t * coef[-1] + coef[-2]
    for c in coef[-3::-1]:
        total = total * t + c
    return total


def half_angle(turns):
    r = turns - ((turns + ROUNDER) - ROUNDER)
    t = r * r
    return r * horner(SIN_COEF, t), horner(COS_COEF, t)


def kernel(
    sizes,
    src_hbm,
    geom_ref,
    cot_ref,
    fidx_ref,
    head_ref,
    table_ref,
    out_ref,
    geo_ref,
    src,
    vecs,
    ctab,
    stab,
    ef,
    eb,
    hpart,
    pairbuf,
    rsbuf,
    gall,
    lmat,
    lmat_t,
    dscr,
    ssend,
    sown,
    sbuf,
    qsend,
    qrecv,
    msend,
    mrecv,
    gsum,
    gbuf,
    src_sem,
    pair_send,
    pair_recv,
    rs_send,
    rs_recv,
    ag_send,
    ag_recv,
    sib_send,
    sib_recv,
    x_send,
    x_recv,
    g_send,
    g_recv,
):
    npan, ndir, nfreq, nf, panels, block = sizes
    nx = ndir // 2
    dirs = HALF // ndir
    own = dirs // npan
    rows = 2 * own
    heads2 = src.shape[1]
    heads = heads2 // 2
    pi = lax.axis_index("panel")
    di = lax.axis_index("dir")
    fi = lax.axis_index("freq")
    x = di // 2
    core = di % 2

    copies = [pltpu.make_async_copy(src_hbm.at[f], src.at[f], src_sem.at[f]) for f in range(nf)]
    for c in copies:
        c.start()

    barrier = pltpu.get_barrier_semaphore()

    def greet_panel(o, carry):
        pl.semaphore_signal(barrier, inc=1, device_id={"panel": (pi + o) % npan}, device_id_type=MESH)
        return carry

    lax.fori_loop(1, npan, greet_panel, 0)
    for b in range(nfreq):

        def greet_dir(o, carry):
            pl.semaphore_signal(
                barrier,
                inc=1,
                device_id={"dir": (di + o) % ndir, "freq": (fi + b) % nfreq},
                device_id_type=MESH,
            )
            return carry

        lax.fori_loop(0 if b else 1, ndir, greet_dir, 0)

    for half in range(dirs // 128):
        row = di * (dirs // 128) + half
        at = pl.ds(half * 128, 128)
        ctab[at, :] = jnp.broadcast_to(table_ref[0, pl.ds(row, 1), :], (128, 128)).T
        stab[at, :] = jnp.broadcast_to(table_ref[1, pl.ds(row, 1), :], (128, 128)).T

    gsum[...] = jnp.zeros(gsum.shape, F32)
    def prepare(f):
        omega = omega_low + omega_span * fidx_ref[f].astype(F32) / FREQS
        om = jnp.full((1, panels), omega, F32)
        k = om * om / gravity
        amp = geom_ref[3:4, :] * jnp.exp(k * geom_ref[2:3, :])
        vecs[f, 0:1, :] = k * geom_ref[0:1, :] * (0.5 / math.pi)
        vecs[f, 1:2, :] = k * geom_ref[1:2, :] * (0.5 / math.pi)
        vecs[f, 2:3, :] = amp
        vecs[f, 3:4, :] = -2.0 * amp
        vecs[f, 4:5, :] = k
        vecs[f, 5:6, :] = 1.0 / amp

    def forward(f, lo, hi):
        some = pl.ds(lo * rows, (hi - lo) * rows)

        def step(b, carry):
            lanes = pl.ds(pl.multiple_of(b * block, block), block)

            for g in range(lo, hi):
                at = pl.ds(g * own, own)
                ct = jnp.concatenate([ctab[at, :]] * (block // 128), axis=1)
                st = jnp.concatenate([stab[at, :]] * (block // 128), axis=1)
                turns = vecs[f, 0:1, lanes] * ct + vecs[f, 1:2, lanes] * st
                s, c = half_angle(turns)
                q = s * vecs[f, 3:4, lanes]
                re = vecs[f, 2:3, lanes] + q * s
                im = q * c
                base = g * rows
                ef[f, pl.ds(base, own), lanes] = re
                ef[f, pl.ds(base + own, own), lanes] = im
                eb[f, pl.ds(base, own), lanes] = re.astype(BF16)
                eb[f, pl.ds(base + own, own), lanes] = im.astype(BF16)
            hpart[f, some] += lax.dot_general(
                eb[f, some, lanes],
                src[f, :, lanes],
                (((1,), (1,)), ((), ())),
                preferred_element_type=F32,
            )
            return carry

        hpart[f, some] = jnp.zeros(((hi - lo) * rows, heads2), F32)
        if lo == 0:
            prepare(f)
            copies[f].wait()
        lax.fori_loop(0, panels // block, step, 0)

    def loop_over(lo, hi, fn):
        def step(o, carry):
            fn(o)
            return carry

        lax.fori_loop(lo, hi, step, 0)

    ring = npan // 2
    side = pi // ring
    away = ring * rows
    far_first = sorted(range(ring), key=lambda o: -min(o, ring - o))

    def rs_size(f):
        return ring if f else npan

    def rs_copy(f, o):
        dest = side * ring + (pi + o) % ring if f else (pi + o) % npan
        return pltpu.make_async_remote_copy(
            src_ref=hpart.at[f, pl.ds(pl.multiple_of(dest * rows, rows), rows)],
            dst_ref=rsbuf.at[f, o],
            send_sem=rs_send.at[f, o],
            recv_sem=rs_recv.at[f, o],
            device_id={"panel": dest},
            device_id_type=MESH,
        )

    def pair_copy(f):
        other = pl.multiple_of((1 - side) * away, away)
        return pltpu.make_async_remote_copy(
            src_ref=hpart.at[f, pl.ds(other, away)],
            dst_ref=pairbuf.at[f],
            send_sem=pair_send.at[f],
            recv_sem=pair_recv.at[f],
            device_id={"panel": (pi + ring) % npan},
            device_id_type=MESH,
        )

    def spread(f):
        pair_copy(f).wait_recv()
        mine = pl.ds(pl.multiple_of(side * away, away), away)
        hpart[f, mine] += pairbuf[f]
        for o in far_first[:-1]:
            rs_copy(f, o).start()

    def ag_copy(f, o):
        dest = (pi + o) % npan
        return pltpu.make_async_remote_copy(
            src_ref=gall.at[f, pi],
            dst_ref=gall.at[f, pi],
            send_sem=ag_send.at[f, o],
            recv_sem=ag_recv.at[f, o],
            device_id={"panel": dest},
            device_id_type=MESH,
        )

    def ag_arrival(f, o):
        origin = (pi - o + npan) % npan
        return pltpu.make_async_remote_copy(
            src_ref=gall.at[f, origin],
            dst_ref=gall.at[f, origin],
            send_sem=ag_send.at[f, o],
            recv_sem=ag_recv.at[f, o],
            device_id={"panel": origin},
            device_id_type=MESH,
        )

    def cotangent(f):
        loop_over(1, rs_size(f), lambda o: rs_copy(f, o).wait_recv())
        total = hpart[f, pl.ds(pl.multiple_of(pi * rows, rows), rows), :]
        for o in range(1, rs_size(f)):
            total = total + rsbuf[f, o]
        top = total[:own]
        low = pltpu.roll(total[own:], heads, 1)
        lane = lax.broadcasted_iota(jnp.int32, (own, heads2), 1)
        first = lane < heads
        sign = jnp.where(first, 1.0, -1.0)
        head = jnp.concatenate([head_ref[...]] * 2, axis=1)
        sb, _ = half_angle(head.astype(F32) * (1.0 / ND))
        cosb = 1.0 - 2.0 * sb * sb
        ids = di * dirs + pi * own + lax.broadcasted_iota(jnp.int32, (own, heads2), 0)
        slope = vecs[f, 4:5, 0:heads2] * (-drift_gain) / math.sqrt(ND)
        along = 2.0 * slope * ctab[pl.ds(pl.multiple_of(pi * own, own), own), :] * sign
        weight = jnp.concatenate([cot_ref[f : f + 1, :]] * 2, axis=1)
        pull = cross_gain * cosb
        hit = jnp.where((ids == head) & first, pull, 0.0)
        hit_far = jnp.where((ids + HALF == head) & first, pull, 0.0)
        near = weight * (along * (top - low) - hit)
        far = weight * (-along * (top + low) - hit_far)
        gall[f, pi] = jnp.concatenate([near, far], axis=1).astype(BF16)
        for near in far_first:
            for o in (near, near + ring):
                if o:
                    ag_copy(f, o).start()

    def gather(f):
        loop_over(1, npan, lambda o: ag_arrival(f, o).wait_recv())

        for g in range(npan):
            near = gall[f, g, :, 0:heads2].astype(F32)
            far = gall[f, g, :, heads2:].astype(F32)
            top = jnp.concatenate([near, far], axis=1)
            low = jnp.concatenate([pltpu.roll(far, heads, 1), -pltpu.roll(near, heads, 1)], axis=1)
            both = jnp.concatenate([top, low], axis=0)
            lmat[f, pl.ds(g * rows, rows), :] = both.astype(BF16)
        for part in range(2 * dirs // 128):
            at = pl.ds(part * 128, 128)
            lmat_t[f, :, at] = lmat[f, at, :].astype(F32).T.astype(BF16)

    sub = 256

    def backward(f, xdest, column, dst):
        j = xdest * 2 + column

        def step(n, carry):
            lanes = pl.ds(pl.multiple_of(j * block + n * sub, sub), sub)
            w = src[f, :, lanes]
            both = jnp.dot(lmat_t[f], eb[f, :, lanes], preferred_element_type=F32)
            dst[:, pl.ds(pl.multiple_of(n * sub, sub), sub)] = both[:heads2] + both[heads2:]
            dscr[...] = jnp.dot(lmat[f], jnp.concatenate([w, w], axis=0), preferred_element_type=F32)

            zero = jnp.zeros((8, sub), F32)
            acc = (zero, zero, zero)
            for g in range(npan):
                base = g * rows
                at = pl.ds(g * own, own)
                ct = jnp.concatenate([ctab[at, :]] * (sub // 128), axis=1)
                st = jnp.concatenate([stab[at, :]] * (sub // 128), axis=1)
                u = dscr[pl.ds(base, own), :]
                v = dscr[pl.ds(base + own, own), :]
                re = ef[f, pl.ds(base, own), lanes]
                im = ef[f, pl.ds(base + own, own), lanes]
                twist = u * im - v * re
                swell = u * re + v * im
                terms = (twist * ct, twist * st, swell)
                acc = tuple(
                    a + sum(t[8 * i : 8 * i + 8] for i in range(own // 8))
                    for a, t in zip(acc, terms)
                )
            qc, qs, rs = acc
            k = vecs[f, 4:5, lanes]
            qc = k * jnp.sum(qc, axis=0, keepdims=True)
            qs = k * jnp.sum(qs, axis=0, keepdims=True)
            rs = jnp.sum(rs, axis=0, keepdims=True)
            for r, value in enumerate((qc, qs, k * rs, rs)):
                gsum[j, pl.ds(4 * n + r, 1), :] += value
            return carry

        lax.fori_loop(0, block // sub, step, 0)

    xp = (x + 1) % nx
    xm = (x + nx - 1) % nx
    x2 = (x + 2) % nx
    order = (x2, xp, xm, x)

    def sib_copy(f, n):
        return pltpu.make_async_remote_copy(
            src_ref=ssend.at[f, n],
            dst_ref=sbuf.at[f, n],
            send_sem=sib_send.at[f, n],
            recv_sem=sib_recv.at[f, n],
            device_id={"dir": x * 2 + (1 - core)},
            device_id_type=MESH,
        )

    upper, lower = pl.ds(0, heads), pl.ds(heads, heads)
    messages = (
        (0, upper, xp),
        (0, lower, xm),
        (1, lower, xp),
        (1, upper, xp),
        (2, upper, xm),
        (2, lower, xm),
    )

    def x_copies(f, m):
        to = messages[m][2]
        return [
            pltpu.make_async_remote_copy(
                src_ref=out_at.at[f, m],
                dst_ref=in_at.at[f, m],
                send_sem=x_send.at[f, m, i],
                recv_sem=x_recv.at[f, m, i],
                device_id={"dir": to * 2 + core},
                device_id_type=MESH,
            )
            for i, (out_at, in_at) in enumerate(((qsend, qrecv), (msend, mrecv)))
        ]

    def block_lanes(n):
        return pl.ds(pl.multiple_of((order[n] * 2 + core) * block, block), block)

    lane = lax.broadcasted_iota(jnp.int32, (8, 128), 1)

    def x_start(f, m):
        n, part, _ = messages[m]
        value = sown[f, n, part] * vecs[f, 5:6, block_lanes(n)]
        top = jnp.maximum(jnp.max(jnp.abs(value), axis=1, keepdims=True), 1e-30)
        level = value * (32000.0 / top)
        level = (level + ROUNDER) - ROUNDER
        qsend[f, m] = level.astype(jnp.int32).astype(jnp.int16)
        unit = jnp.broadcast_to(top * (1.0 / 32000.0), (heads, 128))
        packed = unit[0:8]
        for i in range(1, heads // 8):
            packed = jnp.where(lane >= 16 * i, unit[8 * i : 8 * i + 8], packed)
        msend[f, m] = packed
        for c in x_copies(f, m):
            c.start()

    def x_read(f, m, n):
        level = qrecv[f, m].astype(jnp.int32).astype(F32)
        unit = mrecv[f, m]
        unit = jnp.concatenate(
            [
                jnp.broadcast_to(unit[:, 16 * i : 16 * i + 1], (8, block))
                for i in range(heads // 8)
            ],
            axis=0,
        )
        return level * unit * vecs[f, 2:3, block_lanes(n)]

    def x_wait(f, m):
        for c in x_copies(f, m):
            c.wait_recv()

    def g_copy(b, o):
        to = (di + o) % ndir
        return pltpu.make_async_remote_copy(
            src_ref=gsum.at[to],
            dst_ref=gbuf.at[b, o],
            send_sem=g_send.at[b, o],
            recv_sem=g_recv.at[b, o],
            device_id={"dir": to, "freq": (fi + b) % nfreq},
            device_id_type=MESH,
        )

    def g_start(j, shifts):
        o = (j - di + ndir) % ndir
        for b in shifts:
            g_copy(b, o).start()

    def to_sibling(f, n):
        backward(f, order[n], 1 - core, ssend.at[f, n])
        sib_copy(f, n).start()
        if f == nf - 1:
            g_start(order[n] * 2 + (1 - core), range(nfreq))

    def keep(f, n):
        backward(f, order[n], core, sown.at[f, n])
        if f == nf - 1:
            g_start(order[n] * 2 + core, range(1 if n == 3 else 0, nfreq))

    def join(f, n):
        sib_copy(f, n).wait_recv()
        sown[f, n] += sbuf[f, n]

    def reverse(f, meanwhile=None):
        to_sibling(f, 0)
        keep(f, 0)
        to_sibling(f, 1)
        join(f, 0)
        x_start(f, 0)
        x_start(f, 1)
        keep(f, 1)
        to_sibling(f, 2)
        join(f, 1)
        x_start(f, 2)
        keep(f, 2)
        to_sibling(f, 3)
        join(f, 2)
        x_start(f, 4)
        if meanwhile:
            meanwhile()
        keep(f, 3)

    def relay(f):
        x_wait(f, 0)
        sown[f, 1, upper] += x_read(f, 0, 1)
        x_start(f, 3)
        x_wait(f, 1)
        sown[f, 2, lower] += x_read(f, 1, 2)
        x_start(f, 5)

    def finish(f):
        sib_copy(f, 3).wait_recv()
        for m in (2, 4, 3, 5):
            x_wait(f, m)
        total = sown[f, 3] + sbuf[f, 3]
        out_ref[f, upper] = total[:heads] + x_read(f, 3, 3) + x_read(f, 4, 3)
        out_ref[f, lower] = total[heads:] + x_read(f, 2, 3) + x_read(f, 5, 3)

    def send_sums(half):
        for near in far_first:
            dest = half * ring + (pi + near) % ring
            o = (dest - pi + npan) % npan

            @pl.when(o != 0)
            def _():
                rs_copy(0, o).start()

    middle = npan // 2
    forward(0, 0, middle)
    pl.semaphore_wait(barrier, npan - 1 + nfreq * ndir - 1)
    send_sums(0)
    forward(0, middle, npan)
    send_sums(1)
    forward(1, 0, npan)
    pair_copy(1).start()
    cotangent(0)
    spread(1)
    cotangent(1)
    gather(0)
    reverse(0)
    relay(0)
    gather(1)
    reverse(1, lambda: relay(1))
    finish(0)
    for b in range(nfreq):
        loop_over(0 if b else 1, ndir, lambda o: g_copy(b, o).wait_recv())
    total = gsum[di]
    for b in range(nfreq):
        for o in range(0 if b else 1, ndir):
            total = total + gbuf[b, o]
    for n in range(block // sub):
        here = pl.ds(n * sub, sub)
        area = geom_ref[3:4, pl.ds(pl.multiple_of(di * block + n * sub, sub), sub)]
        geo_ref[0:3, here] = shape_scale * total[4 * n : 4 * n + 3]
        geo_ref[3:4, here] = shape_scale * (total[4 * n + 3 : 4 * n + 4] / area)
    finish(1)

    for f in range(nf):
        if f:
            pair_copy(f).wait_send()
        loop_over(1, rs_size(f), lambda o: rs_copy(f, o).wait_send())
        loop_over(1, npan, lambda o: ag_copy(f, o).wait_send())
        for n in range(4):
            sib_copy(f, n).wait_send()
        for m in range(6):
            for c in x_copies(f, m):
                c.wait_send()
    for b in range(nfreq):
        loop_over(0 if b else 1, ndir, lambda o: g_copy(b, o).wait_send())


def hand_on(out_in, geo_in, out_ref, geo_ref):
    out_ref[...] = out_in[...]
    geo_ref[...] = geo_in[...]


def direction_table():
    angle = np.arange(HALF, dtype=np.float64) * (2.0 * np.pi / ND)
    return np.stack([np.cos(angle), np.sin(angle)]).astype(np.float32).reshape(2, HALF // 128, 128)


def solution(mesh):
    npan, ndir, nfreq = (mesh.shape[a] for a in ("panel", "dir", "freq"))

    def body(sources, panel_geom, drift_cot, freq_index, heading_dir):
        nf, parts, heads, panels = sources.shape
        block = panels // ndir
        dirs = HALF // ndir
        own = dirs // npan
        heads2 = 2 * heads
        sizes = (npan, ndir, nfreq, nf, panels, block)
        dma = pltpu.SemaphoreType.DMA
        vmem = pltpu.VMEM
        out, geo = pl.pallas_call(
            functools.partial(kernel, sizes),
            out_shape=(
                jax.ShapeDtypeStruct((nf, heads2, block), F32),
                jax.ShapeDtypeStruct((4, block), F32),
            ),
            in_specs=[
                pl.BlockSpec(memory_space=pl.ANY),
                pl.BlockSpec(memory_space=vmem),
                pl.BlockSpec(memory_space=vmem),
                pl.BlockSpec(memory_space=pltpu.SMEM),
                pl.BlockSpec(memory_space=vmem),
                pl.BlockSpec(memory_space=vmem),
            ],
            out_specs=(pl.BlockSpec(memory_space=vmem), pl.BlockSpec(memory_space=vmem)),
            scratch_shapes=[
                vmem((nf, heads2, panels), BF16),
                vmem((nf, 8, panels), F32),
                vmem((dirs, 128), F32),
                vmem((dirs, 128), F32),
                vmem((nf, 2 * dirs, panels), F32),
                vmem((nf, 2 * dirs, panels), BF16),
                vmem((nf, 2 * dirs, heads2), F32),
                vmem((nf, dirs, heads2), F32),
                vmem((nf, npan, 2 * own, heads2), F32),
                vmem((nf, npan, own, 2 * heads2), BF16),
                vmem((nf, 2 * dirs, 2 * heads2), BF16),
                vmem((nf, 2 * heads2, 2 * dirs), BF16),
                vmem((2 * dirs, 256), F32),
                vmem((nf, 4, heads2, block), F32),
                vmem((nf, 4, heads2, block), F32),
                vmem((nf, 4, heads2, block), F32),
                vmem((nf, 6, heads, block), jnp.int16),
                vmem((nf, 6, heads, block), jnp.int16),
                vmem((nf, 6, 8, 128), F32),
                vmem((nf, 6, 8, 128), F32),
                vmem((ndir, 8, block // 2), F32),
                vmem((nfreq, ndir, 8, block // 2), F32),
                dma((nf,)),
                dma((nf,)),
                dma((nf,)),
                dma((nf, npan)),
                dma((nf, npan)),
                dma((nf, npan)),
                dma((nf, npan)),
                dma((nf, 4)),
                dma((nf, 4)),
                dma((nf, 6, 2)),
                dma((nf, 6, 2)),
                dma((nfreq, ndir)),
                dma((nfreq, ndir)),
            ],
            compiler_params=pltpu.CompilerParams(
                collective_id=0, has_side_effects=True, vmem_limit_bytes=60 * 1024 * 1024
            ),
        )(
            sources.reshape(nf, heads2, panels),
            panel_geom,
            drift_cot,
            freq_index,
            heading_dir.reshape(1, heads),
            jnp.asarray(direction_table()),
        )
        out, geo = pl.pallas_call(
            hand_on,
            out_shape=(
                jax.ShapeDtypeStruct(out.shape, F32),
                jax.ShapeDtypeStruct(geo.shape, F32),
            ),
        )(out, geo)
        return out.reshape(nf, parts, heads, block), geo

    return jax.shard_map(
        body,
        mesh=mesh,
        in_specs=(
            P("freq", None, None, "panel"),
            P(None, "panel"),
            P("freq", None),
            P("freq"),
            P(),
        ),
        out_specs=(P("freq", None, None, ("panel", "dir")), P(None, ("panel", "dir"))),
        check_vma=False,
    )
```

```python
import functools
import math

import jax
import jax.numpy as jnp
import numpy as np
from jax import lax
from jax.experimental import pallas as pl
from jax.experimental.pallas import tpu as pltpu
from jax.sharding import PartitionSpec as P

ND = 4096
FREQS = 512
HALF = ND // 2

gravity = 9.81
omega_low = 0.6
omega_span = 0.8
drift_gain = 5.0
cross_gain = 0.5
shape_scale = 100.0

MESH = pl.DeviceIdType.MESH
F32 = jnp.float32
BF16 = jnp.bfloat16
ROUNDER = 1.5 * 2.0**23


def fit_even(values, degree):
    nodes = np.cos((2 * np.arange(400) + 1) * np.pi / 800)
    t = (nodes + 1) / 8
    cheb = np.polynomial.chebyshev.Chebyshev.fit(t, values(t), degree, domain=[0, 0.25])
    return [float(np.float32(c)) for c in cheb.convert(kind=np.polynomial.Polynomial).coef]


SIN_COEF = fit_even(lambda t: np.sinc(np.sqrt(t)) * np.pi, 3)
COS_COEF = fit_even(lambda t: np.cos(np.pi * np.sqrt(t)), 3)


def horner(coef, t):
    total = t * coef[-1] + coef[-2]
    for c in coef[-3::-1]:
        total = total * t + c
    return total


def half_angle(turns):
    r = turns - ((turns + ROUNDER) - ROUNDER)
    t = r * r
    return r * horner(SIN_COEF, t), horner(COS_COEF, t)


def kernel(
    sizes,
    src_hbm,
    geom_ref,
    cot_ref,
    fidx_ref,
    head_ref,
    table_ref,
    out_ref,
    geo_ref,
    src,
    vecs,
    ctab,
    stab,
    ef,
    eb,
    hpart,
    pairbuf,
    rsbuf,
    gall,
    lmat,
    lmat_t,
    dscr,
    ssend,
    sown,
    sbuf,
    qsend,
    qrecv,
    msend,
    mrecv,
    gsum,
    gbuf,
    src_sem,
    pair_send,
    pair_recv,
    rs_send,
    rs_recv,
    ag_send,
    ag_recv,
    sib_send,
    sib_recv,
    x_send,
    x_recv,
    g_send,
    g_recv,
):
    npan, ndir, nfreq, nf, panels, block = sizes
    nx = ndir // 2
    dirs = HALF // ndir
    own = dirs // npan
    rows = 2 * own
    heads2 = src.shape[1]
    heads = heads2 // 2
    pi = lax.axis_index("panel")
    di = lax.axis_index("dir")
    fi = lax.axis_index("freq")
    x = di // 2
    core = di % 2

    copies = [pltpu.make_async_copy(src_hbm.at[f], src.at[f], src_sem.at[f]) for f in range(nf)]
    for c in copies:
        c.start()

    barrier = pltpu.get_barrier_semaphore()

    def greet_panel(o, carry):
        pl.semaphore_signal(barrier, inc=1, device_id={"panel": (pi + o) % npan}, device_id_type=MESH)
        return carry

    lax.fori_loop(1, npan, greet_panel, 0)
    for b in range(nfreq):

        def greet_dir(o, carry):
            pl.semaphore_signal(
                barrier,
                inc=1,
                device_id={"dir": (di + o) % ndir, "freq": (fi + b) % nfreq},
                device_id_type=MESH,
            )
            return carry

        lax.fori_loop(0 if b else 1, ndir, greet_dir, 0)

    for half in range(dirs // 128):
        row = di * (dirs // 128) + half
        at = pl.ds(half * 128, 128)
        ctab[at, :] = jnp.broadcast_to(table_ref[0, pl.ds(row, 1), :], (128, 128)).T
        stab[at, :] = jnp.broadcast_to(table_ref[1, pl.ds(row, 1), :], (128, 128)).T

    gsum[...] = jnp.zeros(gsum.shape, F32)
    def prepare(f):
        omega = omega_low + omega_span * fidx_ref[f].astype(F32) / FREQS
        om = jnp.full((1, panels), omega, F32)
        k = om * om / gravity
        amp = geom_ref[3:4, :] * jnp.exp(k * geom_ref[2:3, :])
        vecs[f, 0:1, :] = k * geom_ref[0:1, :] * (0.5 / math.pi)
        vecs[f, 1:2, :] = k * geom_ref[1:2, :] * (0.5 / math.pi)
        vecs[f, 2:3, :] = amp
        vecs[f, 3:4, :] = -2.0 * amp
        vecs[f, 4:5, :] = k
        vecs[f, 5:6, :] = 1.0 / amp

    def forward(f, lo, count, first):
        some = pl.ds(pl.multiple_of(lo * rows, count * rows), count * rows)

        def step(b, carry):
            lanes = pl.ds(pl.multiple_of(b * block, block), block)

            for g in range(count):
                at = pl.ds(pl.multiple_of((lo + g) * own, own), own)
                ct = jnp.concatenate([ctab[at, :]] * (block // 128), axis=1)
                st = jnp.concatenate([stab[at, :]] * (block // 128), axis=1)
                turns = vecs[f, 0:1, lanes] * ct + vecs[f, 1:2, lanes] * st
                s, c = half_angle(turns)
                q = s * vecs[f, 3:4, lanes]
                re = vecs[f, 2:3, lanes] + q * s
                im = q * c
                base = pl.multiple_of((lo + g) * rows, rows)
                ef[f, pl.ds(base, own), lanes] = re
                ef[f, pl.ds(base + own, own), lanes] = im
                eb[f, pl.ds(base, own), lanes] = re.astype(BF16)
                eb[f, pl.ds(base + own, own), lanes] = im.astype(BF16)
            hpart[f, some] += lax.dot_general(
                eb[f, some, lanes],
                src[f, :, lanes],
                (((1,), (1,)), ((), ())),
                preferred_element_type=F32,
            )
            return carry

        hpart[f, some] = jnp.zeros((count * rows, heads2), F32)
        if first:
            prepare(f)
            copies[f].wait()
        lax.fori_loop(0, panels // block, step, 0)

    def loop_over(lo, hi, fn):
        def step(o, carry):
            fn(o)
            return carry

        lax.fori_loop(lo, hi, step, 0)

    ring = npan // 2
    side = pi // ring
    away = ring * rows
    far_first = sorted(range(ring), key=lambda o: -min(o, ring - o))

    def rs_size(f):
        return ring if f else npan

    def rs_copy(f, o):
        dest = side * ring + (pi + o) % ring if f else (pi + o) % npan
        return pltpu.make_async_remote_copy(
            src_ref=hpart.at[f, pl.ds(pl.multiple_of(dest * rows, rows), rows)],
            dst_ref=rsbuf.at[f, o],
            send_sem=rs_send.at[f, o],
            recv_sem=rs_recv.at[f, o],
            device_id={"panel": dest},
            device_id_type=MESH,
        )

    def pair_copy(f):
        other = pl.multiple_of((1 - side) * away, away)
        return pltpu.make_async_remote_copy(
            src_ref=hpart.at[f, pl.ds(other, away)],
            dst_ref=pairbuf.at[f],
            send_sem=pair_send.at[f],
            recv_sem=pair_recv.at[f],
            device_id={"panel": (pi + ring) % npan},
            device_id_type=MESH,
        )

    def spread(f):
        pair_copy(f).wait_recv()
        mine = pl.ds(pl.multiple_of(side * away, away), away)
        hpart[f, mine] += pairbuf[f]
        for o in far_first[:-1]:
            rs_copy(f, o).start()

    def ag_copy(f, o):
        dest = (pi + o) % npan
        return pltpu.make_async_remote_copy(
            src_ref=gall.at[f, pi],
            dst_ref=gall.at[f, pi],
            send_sem=ag_send.at[f, o],
            recv_sem=ag_recv.at[f, o],
            device_id={"panel": dest},
            device_id_type=MESH,
        )

    def ag_arrival(f, o):
        origin = (pi - o + npan) % npan
        return pltpu.make_async_remote_copy(
            src_ref=gall.at[f, origin],
            dst_ref=gall.at[f, origin],
            send_sem=ag_send.at[f, o],
            recv_sem=ag_recv.at[f, o],
            device_id={"panel": origin},
            device_id_type=MESH,
        )

    def cotangent(f):
        loop_over(1, rs_size(f), lambda o: rs_copy(f, o).wait_recv())
        total = hpart[f, pl.ds(pl.multiple_of(pi * rows, rows), rows), :]
        for o in range(1, rs_size(f)):
            total = total + rsbuf[f, o]
        top = total[:own]
        low = pltpu.roll(total[own:], heads, 1)
        lane = lax.broadcasted_iota(jnp.int32, (own, heads2), 1)
        first = lane < heads
        sign = jnp.where(first, 1.0, -1.0)
        head = jnp.concatenate([head_ref[...]] * 2, axis=1)
        sb, _ = half_angle(head.astype(F32) * (1.0 / ND))
        cosb = 1.0 - 2.0 * sb * sb
        ids = di * dirs + pi * own + lax.broadcasted_iota(jnp.int32, (own, heads2), 0)
        slope = vecs[f, 4:5, 0:heads2] * (-drift_gain) / math.sqrt(ND)
        along = 2.0 * slope * ctab[pl.ds(pl.multiple_of(pi * own, own), own), :] * sign
        weight = jnp.concatenate([cot_ref[f : f + 1, :]] * 2, axis=1)
        pull = cross_gain * cosb
        hit = jnp.where((ids == head) & first, pull, 0.0)
        hit_far = jnp.where((ids + HALF == head) & first, pull, 0.0)
        near = weight * (along * (top - low) - hit)
        far = weight * (-along * (top + low) - hit_far)
        gall[f, pi] = jnp.concatenate([near, far], axis=1).astype(BF16)
        for near in far_first:
            for o in (near, near + ring):
                if o:
                    ag_copy(f, o).start()

    def gather(f):
        loop_over(1, npan, lambda o: ag_arrival(f, o).wait_recv())

        for g in range(npan):
            near = gall[f, g, :, 0:heads2].astype(F32)
            far = gall[f, g, :, heads2:].astype(F32)
            top = jnp.concatenate([near, far], axis=1)
            low = jnp.concatenate([pltpu.roll(far, heads, 1), -pltpu.roll(near, heads, 1)], axis=1)
            both = jnp.concatenate([top, low], axis=0)
            lmat[f, pl.ds(g * rows, rows), :] = both.astype(BF16)
        for part in range(2 * dirs // 128):
            at = pl.ds(part * 128, 128)
            lmat_t[f, :, at] = lmat[f, at, :].astype(F32).T.astype(BF16)

    sub = 256

    def backward(f, xdest, column, dst):
        j = xdest * 2 + column

        def step(n, carry):
            lanes = pl.ds(pl.multiple_of(j * block + n * sub, sub), sub)
            w = src[f, :, lanes]
            both = jnp.dot(lmat_t[f], eb[f, :, lanes], preferred_element_type=F32)
            dst[:, pl.ds(pl.multiple_of(n * sub, sub), sub)] = both[:heads2] + both[heads2:]
            dscr[...] = jnp.dot(lmat[f], jnp.concatenate([w, w], axis=0), preferred_element_type=F32)

            zero = jnp.zeros((8, sub), F32)
            acc = (zero, zero, zero)
            for g in range(npan):
                base = g * rows
                at = pl.ds(g * own, own)
                ct = jnp.concatenate([ctab[at, :]] * (sub // 128), axis=1)
                st = jnp.concatenate([stab[at, :]] * (sub // 128), axis=1)
                u = dscr[pl.ds(base, own), :]
                v = dscr[pl.ds(base + own, own), :]
                re = ef[f, pl.ds(base, own), lanes]
                im = ef[f, pl.ds(base + own, own), lanes]
                twist = u * im - v * re
                swell = u * re + v * im
                terms = (twist * ct, twist * st, swell)
                acc = tuple(
                    a + sum(t[8 * i : 8 * i + 8] for i in range(own // 8))
                    for a, t in zip(acc, terms)
                )
            qc, qs, rs = acc
            k = vecs[f, 4:5, lanes]
            qc = k * jnp.sum(qc, axis=0, keepdims=True)
            qs = k * jnp.sum(qs, axis=0, keepdims=True)
            rs = jnp.sum(rs, axis=0, keepdims=True)
            for r, value in enumerate((qc, qs, k * rs, rs)):
                gsum[j, pl.ds(4 * n + r, 1), :] += value
            return carry

        lax.fori_loop(0, block // sub, step, 0)

    xp = (x + 1) % nx
    xm = (x + nx - 1) % nx
    x2 = (x + 2) % nx
    order = (x2, xp, xm, x)

    def sib_copy(f, n):
        return pltpu.make_async_remote_copy(
            src_ref=ssend.at[f, n],
            dst_ref=sbuf.at[f, n],
            send_sem=sib_send.at[f, n],
            recv_sem=sib_recv.at[f, n],
            device_id={"dir": x * 2 + (1 - core)},
            device_id_type=MESH,
        )

    upper, lower = pl.ds(0, heads), pl.ds(heads, heads)
    messages = (
        (0, upper, xp),
        (0, lower, xm),
        (1, lower, xp),
        (1, upper, xp),
        (2, upper, xm),
        (2, lower, xm),
    )

    def x_copies(f, m):
        to = messages[m][2]
        return [
            pltpu.make_async_remote_copy(
                src_ref=out_at.at[f, m],
                dst_ref=in_at.at[f, m],
                send_sem=x_send.at[f, m, i],
                recv_sem=x_recv.at[f, m, i],
                device_id={"dir": to * 2 + core},
                device_id_type=MESH,
            )
            for i, (out_at, in_at) in enumerate(((qsend, qrecv), (msend, mrecv)))
        ]

    def block_lanes(n):
        return pl.ds(pl.multiple_of((order[n] * 2 + core) * block, block), block)

    lane = lax.broadcasted_iota(jnp.int32, (8, 128), 1)

    def x_start(f, m):
        n, part, _ = messages[m]
        value = sown[f, n, part] * vecs[f, 5:6, block_lanes(n)]
        top = jnp.maximum(jnp.max(jnp.abs(value), axis=1, keepdims=True), 1e-30)
        level = value * (32000.0 / top)
        level = (level + ROUNDER) - ROUNDER
        qsend[f, m] = level.astype(jnp.int32).astype(jnp.int16)
        unit = jnp.broadcast_to(top * (1.0 / 32000.0), (heads, 128))
        packed = unit[0:8]
        for i in range(1, heads // 8):
            packed = jnp.where(lane >= 16 * i, unit[8 * i : 8 * i + 8], packed)
        msend[f, m] = packed
        for c in x_copies(f, m):
            c.start()

    def x_read(f, m, n):
        level = qrecv[f, m].astype(jnp.int32).astype(F32)
        unit = mrecv[f, m]
        unit = jnp.concatenate(
            [
                jnp.broadcast_to(unit[:, 16 * i : 16 * i + 1], (8, block))
                for i in range(heads // 8)
            ],
            axis=0,
        )
        return level * unit * vecs[f, 2:3, block_lanes(n)]

    def x_wait(f, m):
        for c in x_copies(f, m):
            c.wait_recv()

    def g_copy(b, o):
        to = (di + o) % ndir
        return pltpu.make_async_remote_copy(
            src_ref=gsum.at[to],
            dst_ref=gbuf.at[b, o],
            send_sem=g_send.at[b, o],
            recv_sem=g_recv.at[b, o],
            device_id={"dir": to, "freq": (fi + b) % nfreq},
            device_id_type=MESH,
        )

    def g_start(j, shifts):
        o = (j - di + ndir) % ndir
        for b in shifts:
            g_copy(b, o).start()

    def to_sibling(f, n):
        backward(f, order[n], 1 - core, ssend.at[f, n])
        sib_copy(f, n).start()
        if f == nf - 1:
            g_start(order[n] * 2 + (1 - core), range(nfreq))

    def keep(f, n):
        backward(f, order[n], core, sown.at[f, n])
        if f == nf - 1:
            g_start(order[n] * 2 + core, range(1 if n == 3 else 0, nfreq))

    def join(f, n):
        sib_copy(f, n).wait_recv()
        sown[f, n] += sbuf[f, n]

    def reverse(f, meanwhile=None):
        to_sibling(f, 0)
        keep(f, 0)
        to_sibling(f, 1)
        join(f, 0)
        x_start(f, 0)
        x_start(f, 1)
        keep(f, 1)
        to_sibling(f, 2)
        join(f, 1)
        x_start(f, 2)
        keep(f, 2)
        to_sibling(f, 3)
        join(f, 2)
        x_start(f, 4)
        if meanwhile:
            meanwhile()
        keep(f, 3)

    def relay(f):
        x_wait(f, 0)
        sown[f, 1, upper] += x_read(f, 0, 1)
        x_start(f, 3)
        x_wait(f, 1)
        sown[f, 2, lower] += x_read(f, 1, 2)
        x_start(f, 5)

    def finish(f):
        sib_copy(f, 3).wait_recv()
        for m in (2, 4, 3, 5):
            x_wait(f, m)
        total = sown[f, 3] + sbuf[f, 3]
        out_ref[f, upper] = total[:heads] + x_read(f, 3, 3) + x_read(f, 4, 3)
        out_ref[f, lower] = total[heads:] + x_read(f, 2, 3) + x_read(f, 5, 3)

    def send_sums(half):
        for near in far_first:
            dest = half * ring + (pi + near) % ring
            o = (dest - pi + npan) % npan

            @pl.when(o != 0)
            def _():
                rs_copy(0, o).start()

    middle = npan // 2
    forward(0, 0, middle, True)
    pl.semaphore_wait(barrier, npan - 1 + nfreq * ndir - 1)
    send_sums(0)
    forward(0, middle, middle, False)
    send_sums(1)
    forward(1, (1 - side) * middle, middle, True)
    pair_copy(1).start()
    forward(1, side * middle, middle, False)
    cotangent(0)
    spread(1)
    cotangent(1)
    gather(0)
    reverse(0)
    relay(0)
    gather(1)
    reverse(1, lambda: relay(1))
    finish(0)
    for b in range(nfreq):
        loop_over(0 if b else 1, ndir, lambda o: g_copy(b, o).wait_recv())
    total = gsum[di]
    for b in range(nfreq):
        for o in range(0 if b else 1, ndir):
            total = total + gbuf[b, o]
    for n in range(block // sub):
        here = pl.ds(n * sub, sub)
        area = geom_ref[3:4, pl.ds(pl.multiple_of(di * block + n * sub, sub), sub)]
        geo_ref[0:3, here] = shape_scale * total[4 * n : 4 * n + 3]
        geo_ref[3:4, here] = shape_scale * (total[4 * n + 3 : 4 * n + 4] / area)
    finish(1)

    for f in range(nf):
        if f:
            pair_copy(f).wait_send()
        loop_over(1, rs_size(f), lambda o: rs_copy(f, o).wait_send())
        loop_over(1, npan, lambda o: ag_copy(f, o).wait_send())
        for n in range(4):
            sib_copy(f, n).wait_send()
        for m in range(6):
            for c in x_copies(f, m):
                c.wait_send()
    for b in range(nfreq):
        loop_over(0 if b else 1, ndir, lambda o: g_copy(b, o).wait_send())


def hand_on(out_in, geo_in, out_ref, geo_ref):
    out_ref[...] = out_in[...]
    geo_ref[...] = geo_in[...]


def direction_table():
    angle = np.arange(HALF, dtype=np.float64) * (2.0 * np.pi / ND)
    return np.stack([np.cos(angle), np.sin(angle)]).astype(np.float32).reshape(2, HALF // 128, 128)


def solution(mesh):
    npan, ndir, nfreq = (mesh.shape[a] for a in ("panel", "dir", "freq"))

    def body(sources, panel_geom, drift_cot, freq_index, heading_dir):
        nf, parts, heads, panels = sources.shape
        block = panels // ndir
        dirs = HALF // ndir
        own = dirs // npan
        heads2 = 2 * heads
        sizes = (npan, ndir, nfreq, nf, panels, block)
        dma = pltpu.SemaphoreType.DMA
        vmem = pltpu.VMEM
        out, geo = pl.pallas_call(
            functools.partial(kernel, sizes),
            out_shape=(
                jax.ShapeDtypeStruct((nf, heads2, block), F32),
                jax.ShapeDtypeStruct((4, block), F32),
            ),
            in_specs=[
                pl.BlockSpec(memory_space=pl.ANY),
                pl.BlockSpec(memory_space=vmem),
                pl.BlockSpec(memory_space=vmem),
                pl.BlockSpec(memory_space=pltpu.SMEM),
                pl.BlockSpec(memory_space=vmem),
                pl.BlockSpec(memory_space=vmem),
            ],
            out_specs=(pl.BlockSpec(memory_space=vmem), pl.BlockSpec(memory_space=vmem)),
            scratch_shapes=[
                vmem((nf, heads2, panels), BF16),
                vmem((nf, 8, panels), F32),
                vmem((dirs, 128), F32),
                vmem((dirs, 128), F32),
                vmem((nf, 2 * dirs, panels), F32),
                vmem((nf, 2 * dirs, panels), BF16),
                vmem((nf, 2 * dirs, heads2), F32),
                vmem((nf, dirs, heads2), F32),
                vmem((nf, npan, 2 * own, heads2), F32),
                vmem((nf, npan, own, 2 * heads2), BF16),
                vmem((nf, 2 * dirs, 2 * heads2), BF16),
                vmem((nf, 2 * heads2, 2 * dirs), BF16),
                vmem((2 * dirs, 256), F32),
                vmem((nf, 4, heads2, block), F32),
                vmem((nf, 4, heads2, block), F32),
                vmem((nf, 4, heads2, block), F32),
                vmem((nf, 6, heads, block), jnp.int16),
                vmem((nf, 6, heads, block), jnp.int16),
                vmem((nf, 6, 8, 128), F32),
                vmem((nf, 6, 8, 128), F32),
                vmem((ndir, 8, block // 2), F32),
                vmem((nfreq, ndir, 8, block // 2), F32),
                dma((nf,)),
                dma((nf,)),
                dma((nf,)),
                dma((nf, npan)),
                dma((nf, npan)),
                dma((nf, npan)),
                dma((nf, npan)),
                dma((nf, 4)),
                dma((nf, 4)),
                dma((nf, 6, 2)),
                dma((nf, 6, 2)),
                dma((nfreq, ndir)),
                dma((nfreq, ndir)),
            ],
            compiler_params=pltpu.CompilerParams(
                collective_id=0, has_side_effects=True, vmem_limit_bytes=60 * 1024 * 1024
            ),
        )(
            sources.reshape(nf, heads2, panels),
            panel_geom,
            drift_cot,
            freq_index,
            heading_dir.reshape(1, heads),
            jnp.asarray(direction_table()),
        )
        out, geo = pl.pallas_call(
            hand_on,
            out_shape=(
                jax.ShapeDtypeStruct(out.shape, F32),
                jax.ShapeDtypeStruct(geo.shape, F32),
            ),
        )(out, geo)
        return out.reshape(nf, parts, heads, block), geo

    return jax.shard_map(
        body,
        mesh=mesh,
        in_specs=(
            P("freq", None, None, "panel"),
            P(None, "panel"),
            P("freq", None),
            P("freq"),
            P(),
        ),
        out_specs=(P("freq", None, None, ("panel", "dir")), P(None, ("panel", "dir"))),
        check_vma=False,
    )
```
